512 devices in a mesh: dom: 32 (over x, y, core), cls: 16 (over z).
Axes of the slice: x: 4, y: 4, z: 16, core: 2. Of those that a mesh axis runs over, the one named last changes fastest.
Arguments:
- particles: bfloat16 [4096, 128, 128], P(('dom', 'cls')), may hold values from -640 to 640
- centers: int32 [4096, 2], P(('dom', 'cls')), may hold values from -3 to 3
- rot_prior: int32 [4096], P(('dom', 'cls')), may hold values from 0 to 3
- groups: int32 [4096, 2], P(('dom', 'cls')), may hold values from 0 to 15, all different within a row; in each aligned block of 8 rows (0 to 7, 8 to 15, ...) at most 2 rows name the same one
- references: bfloat16 [320, 4, 16384], P('cls', None, 'dom'), may hold values from -1 to 1
Outputs:
- class_sums: float32 [16384, 320, 4], P('dom', 'cls')
- log_evidence: float32 [4096], P(('dom', 'cls'))
The draws below stay inside these ranges and needn't reach their ends.
Inputs may be any that keep to these rules, and one draw needn't show every extreme that they name: `groups`: within the 8 rows of one device no class group is named by more than 2 particles, and the lists of one particle are distinct.
All inputs are finite; a program needn't handle non-finite values.
Results may differ from the reference program's by a relative error of at most 0.017.
Values may be sent and summed in bfloat16 or wider, within the bound.
A program may use at most 64 MiB of HBM per device.

```python
import math
import jax
import jax.numpy as jnp
import numpy as np
from jax import lax

H = 128
W = 128
PIX = 16384
PART_DEV = 8
TOPG = 2
CLS_GRP = 20
ROT = 4
MAXC = 3
CAP = 2
PARTICLES = 4096
CLASSES = 320
N_CLS = 16


def draw_centers(key, part):
    return jax.random.randint(jax.random.fold_in(key, 11), (PARTICLES, 2), -MAXC, MAXC + 1).astype(jnp.int32)


def draw_references(key, part):
    base = jnp.clip(jax.random.normal(jax.random.fold_in(key, 12), (CLASSES, ROT, PIX), jnp.float32), -5.0, 5.0)
    return (base / jnp.sqrt(float(PIX))).astype(jnp.bfloat16)


def draw_particles(key, part):
    base = jnp.clip(jax.random.normal(jax.random.fold_in(key, 14), (PARTICLES, H, W), jnp.float32), -5.0, 5.0)
    return base.astype(jnp.bfloat16)


def with_ends(values, rng, least, high):
    extent = values.shape
    index_at = [jax.random.randint(jax.random.fold_in(rng, axis), (), 0, extent[axis]) for axis in range(len(extent))]
    values = values.at[tuple(index_at)].set(least)
    longest = extent.index(max(extent))
    index_at[longest] = (index_at[longest] + 1) % extent[longest]
    return values.at[tuple(index_at)].set(high)


def assign_block(rng, own, number, rows, number_of, top, most, slope):
    order = jax.random.permutation(rng, number_of)
    packed, ordinary = portions_of(number_of, rows * top, most, slope, True), portions_of(number_of, rows * top, most, slope, False)
    places = jnp.arange(number_of)

    def named(lengths, turn):
        used = int((lengths > 0).sum())
        fixed = max(1, used // 4)
        passed = fixed + (places - fixed + turn * (used - fixed)) % max(1, number_of - fixed)
        return jnp.zeros((number_of,), jnp.int32).at[order[jnp.where(places < fixed, places, passed)]].set(jnp.asarray(lengths, jnp.int32))

    lengths = jnp.where(number % 4 == 0, named(packed, number // 4), named(ordinary, number - number // 4 - 1))
    mixed = jax.random.permutation(jax.random.fold_in(own, 3), number_of)
    donor, sink = mixed[0:number_of // 2 * 2:2], mixed[1:number_of // 2 * 2:2]
    slack = jnp.minimum(lengths[donor] - 1, most - lengths[sink]) // 2
    slack = jnp.where((donor == order[0]) | (sink == order[0]) | (lengths[sink] == 0), 0, jnp.maximum(slack, 0))
    passed = jax.random.randint(jax.random.fold_in(own, 4), (number_of // 2,), 0, 1 << 20) % (slack + 1)
    lengths = lengths.at[donor].add(-passed).at[sink].add(passed)
    labels = jnp.searchsorted(jnp.cumsum(lengths), jnp.arange(rows * top), side="right").astype(jnp.int32)
    grid = labels.reshape(top, rows).T
    grid = grid[jax.random.permutation(jax.random.fold_in(own, 1), rows)]
    turn = jax.random.randint(jax.random.fold_in(own, 2), (rows, 1), 0, top)
    return jnp.take_along_axis(grid, (jnp.arange(top)[None, :] + turn) % top, axis=1)


def portions_of(amount, total, limit, skew, full):
    loads = [(1 << 20) // math.isqrt(standing ** skew) + 1 for standing in range(1, amount + 1)]
    largest = limit if full else min(limit, max(-(-total // amount), total * loads[0] // sum(loads)))
    least = 1 if total - largest >= amount - 1 else 0
    given, spare = [largest] + [least] * (amount - 1), total - largest - least * (amount - 1)
    while spare > 0:
        candidates = [i for i in range(1, amount) if given[i] < largest] or [i for i in range(1, amount) if given[i] < limit]
        whole, budget = sum([loads[i] for i in candidates]), spare
        for i in candidates:
            more = min(limit - given[i], max(1, budget * loads[i] // whole), spare)
            given[i] = given[i] + more
            spare = spare - more
    return np.array(given)


def setup_inputs(seed: int = 0) -> dict:
    splits = jax.random.split(jax.random.key(seed), 6)
    particles = draw_particles(jax.random.fold_in(splits[5], 71), 0)
    centers = draw_centers(jax.random.fold_in(splits[5], 71), 0)
    rot_prior = with_ends(jax.random.randint(splits[2], (PARTICLES,), 0, ROT), jax.random.fold_in(splits[2], 1), 0, ROT - 1).astype(jnp.int32)
    groups_keys = jax.random.split(jax.random.fold_in(splits[3], 1), PARTICLES // PART_DEV)
    groups_turns = jax.random.permutation(jax.random.fold_in(splits[3], 3), PARTICLES // PART_DEV)
    groups = jax.vmap(lambda own, number: assign_block(jax.random.fold_in(splits[3], 2), own, number, PART_DEV, N_CLS, TOPG, CAP, 2))(groups_keys, groups_turns).reshape((PARTICLES, TOPG))
    references = draw_references(jax.random.fold_in(splits[5], 71), 0)
    return {"particles": particles, "centers": centers, "rot_prior": rot_prior, "groups": groups, "references": references}


LAMBDA = 1.0


def recenter(image, offset):
    rows = jnp.arange(H, dtype=jnp.int32)
    cols = jnp.arange(W, dtype=jnp.int32)
    row_sel = (rows[None, :] == rows[:, None] + offset[0]).astype(jnp.bfloat16)
    col_sel = (cols[None, :] == cols[:, None] + offset[1]).astype(jnp.bfloat16)
    moved = jnp.dot(row_sel, image, preferred_element_type=jnp.float32).astype(jnp.bfloat16)
    return jnp.dot(moved, col_sel.T, preferred_element_type=jnp.float32).astype(jnp.bfloat16)


def windows(image):
    padded = jnp.pad(image, 1)
    planes = []
    for w in range(9):
        shift_horizontal = w // 3 - 1
        shift_vertical = w % 3 - 1
        planes.append(padded[1 + shift_horizontal:1 + shift_horizontal + H, 1 + shift_vertical:1 + shift_vertical + W].reshape(PIX))
    return jnp.stack(planes)


def reference(particles, centers, rot_prior, groups, references):
    reference_indices = CLS_GRP * ROT
    refs_grp = references.reshape(N_CLS, reference_indices, PIX)
    refs_f = refs_grp.astype(jnp.float32)
    norms = jnp.einsum('gjp,gjp->gj', refs_f, refs_f)
    rot_of = (jnp.arange(reference_indices, dtype=jnp.int32) % ROT).astype(jnp.float32)
    block_tile = PART_DEV * N_CLS
    blocks = PARTICLES // block_tile

    def one_particle(partial_value, idx):
        xw = windows(recenter(particles[idx], centers[idx]))
        prior = rot_prior[idx].astype(jnp.float32)
        delta = jnp.abs(rot_of - prior)
        dist = jnp.minimum(delta, ROT - delta)
        logs = []
        for t in range(TOPG):
            g = groups[idx, t]
            panel = lax.dynamic_index_in_dim(refs_grp, g, 0, keepdims=False)
            score = lax.dot_general(xw, panel, (((1,), (1,)), ((), ())), preferred_element_type=jnp.float32)
            nrm = lax.dynamic_index_in_dim(norms, g, 0, keepdims=False)
            logs.append(score - 0.5 * nrm[None, :] - LAMBDA * dist[None, :] ** 2)
        top = jnp.max(jnp.stack([jnp.max(v) for v in logs]))
        total = sum(jnp.sum(jnp.exp(v - top)) for v in logs)
        evidence = top + jnp.log(total)
        for t in range(TOPG):
            g = groups[idx, t]
            post = jnp.exp(logs[t] - evidence).astype(jnp.bfloat16)
            contrib = lax.dot_general(xw, post, (((0,), (0,)), ((), ())), preferred_element_type=jnp.float32)
            partial_value = partial_value.at[g].add(contrib)
        return partial_value, evidence

    def one_block(total, b):
        start = b * block_tile
        idxs = start + jnp.arange(block_tile, dtype=jnp.int32)
        partial0 = jnp.zeros((N_CLS, PIX, reference_indices), jnp.float32)
        partial_value, evid = lax.scan(one_particle, partial0, idxs)
        rounded = lax.optimization_barrier(partial_value.astype(jnp.bfloat16))
        return total + rounded.astype(jnp.float32), evid

    total0 = jnp.zeros((N_CLS, PIX, reference_indices), jnp.float32)
    total, evid = lax.scan(one_block, total0, jnp.arange(blocks, dtype=jnp.int32))
    sums = total.reshape(N_CLS, PIX, CLS_GRP, ROT).transpose(1, 0, 2, 3).reshape(PIX, CLASSES, ROT)
    return sums, evid.reshape(PARTICLES)
```

```python
import functools

import jax
import jax.numpy as jnp
from jax import lax
from jax.experimental import pallas as pl
from jax.experimental.pallas import tpu as pltpu
from jax.sharding import PartitionSpec as P

LAMBDA = 1.0
NEG_BIG = -1e30
LANES = 128
VMEM = pl.BlockSpec(memory_space=pltpu.VMEM)
MESH = pl.DeviceIdType.MESH


def remote(src, dst, send_sem, recv_sem, peer):
    return pltpu.make_async_remote_copy(
        src_ref=src, dst_ref=dst, send_sem=send_sem, recv_sem=recv_sem, device_id=peer, device_id_type=MESH
    )


def greet(dom, ring):
    barrier = pltpu.get_barrier_semaphore()
    total = 0
    if dom:
        me = lax.axis_index("dom")

        def one(k, carry):
            pl.semaphore_signal(barrier, inc=1, device_id={"dom": lax.rem(me + k, dom)}, device_id_type=MESH)
            return carry

        lax.fori_loop(1, dom, one, 0)
        total += dom - 1
    if ring:
        z = lax.axis_index("cls")
        for step in (1, ring - 1):
            pl.semaphore_signal(barrier, inc=1, device_id={"cls": lax.rem(z + step, ring)}, device_id_type=MESH)
        total += 2
    pl.semaphore_wait(barrier, total)


def chunks(blocks):
    half = (blocks + 1) // 2
    return [(0, half), (half, blocks - half)]


def spread_kernel(dom, ring, refs, imgs, all_refs, all_imgs, rs, rr, ls, lr, ds, dr, local):
    d = lax.axis_index("dom")
    z = lax.axis_index("cls")
    right, left = lax.rem(z + 1, ring), lax.rem(z + ring - 1, ring)
    greet(dom, ring)
    parts = chunks(refs.shape[0])
    steps_r = ring // 2
    steps_l = ring - 1 - steps_r
    own = pltpu.make_async_copy(refs, all_refs.at[z], local.at[0])
    own.start()
    mine = pltpu.make_async_copy(imgs.at[d], all_imgs.at[d], local.at[1])
    mine.start()

    def hop(step, c, to_right):
        first, size = parts[c]
        piece = lax.rem(z + ring - step, ring) if to_right else lax.rem(z + step, ring)
        block = all_refs.at[piece, pl.ds(first, size)]
        src = refs.at[pl.ds(first, size)] if step == 0 else block
        send, recv = (rs, rr) if to_right else (ls, lr)
        return remote(src, block, send.at[step, c], recv.at[step, c], {"cls": right if to_right else left})

    sent = {}
    for c in range(2):
        for to_right in (True, False):
            sent[0, c, to_right] = hop(0, c, to_right)
            sent[0, c, to_right].start()

    def strip(k):
        peer = lax.rem(d + k, dom)
        return remote(imgs.at[peer], all_imgs.at[d], ds.at[k], dr.at[k], {"dom": peer})

    def start(k, carry):
        strip(k).start()
        return carry

    def finish(k, carry):
        strip(k).wait()
        return carry

    lax.fori_loop(1, dom, start, 0)
    for step in range(1, steps_r):
        for c in range(2):
            for to_right in (True, False):
                if step < (steps_r if to_right else steps_l):
                    sent[step - 1, c, to_right].wait_recv()
                    sent[step, c, to_right] = hop(step, c, to_right)
                    sent[step, c, to_right].start()
    for c in range(2):
        sent[steps_r - 1, c, True].wait_recv()
        sent[steps_l - 1, c, False].wait_recv()
    lax.fori_loop(1, dom, finish, 0)
    for copy in sent.values():
        copy.wait_send()
    own.wait()
    mine.wait()


def spread(dom, ring, refs, imgs):
    half = ring // 2
    sem = pltpu.SemaphoreType.DMA
    return pl.pallas_call(
        functools.partial(spread_kernel, dom, ring),
        out_shape=(
            jax.ShapeDtypeStruct((ring,) + refs.shape, refs.dtype),
            jax.ShapeDtypeStruct(imgs.shape, imgs.dtype),
        ),
        in_specs=[VMEM] * 2,
        out_specs=(VMEM, VMEM),
        scratch_shapes=[sem((half, 2))] * 4 + [sem((dom,)), sem((dom,)), sem((2,))],
        compiler_params=pltpu.CompilerParams(collective_id=0, has_side_effects=True),
    )(refs, imgs)


def score_kernel(groups, dim_j, refs, imgs, meta, shifted, out, score, bias):
    dom, strip, count, width = imgs.shape
    own_rows = strip - 3
    slots = dom * count
    lane = lax.broadcasted_iota(jnp.int32, (slots, width), 1)
    for h in range(own_rows + 2):
        mid = imgs[:, h].astype(jnp.float32).reshape(slots, width)
        before = jnp.where(lane == 0, 0.0, pltpu.roll(mid, 1, axis=1))
        after = jnp.where(lane == width - 1, 0.0, pltpu.roll(mid, width - 1, axis=1))
        for sy, plane in enumerate((before, mid, after)):
            plane = plane.astype(jnp.bfloat16)
            for sx in range(3):
                r = h - sx
                if 0 <= r < own_rows:
                    shifted[3 * sx + sy, :, r * width:(r + 1) * width] = plane
    names = [jnp.broadcast_to(meta[t:t + 1, :], (dim_j, slots)) for t in range(2)]

    def add_norm(g, carry):
        rows = pl.ds(pl.multiple_of(g * dim_j, 16), dim_j)
        block = refs[rows, :].astype(jnp.float32)
        norm = jnp.sum(block * block, axis=1, keepdims=True)
        for t in range(2):
            bias[t] = jnp.where(names[t] == g, -0.5 * norm, bias[t])
        return carry

    bias[...] = jnp.zeros_like(bias)
    lax.fori_loop(0, groups, add_norm, 0)

    def one(w, carry):
        score[...] = lax.dot_general(
            refs[...], shifted[w], (((1,), (1,)), ((), ())), preferred_element_type=jnp.float32
        )
        for t in range(2):
            picked = jnp.zeros((dim_j, slots), jnp.float32)
            for g in range(groups):
                picked = jnp.where(names[t] == g, score[g * dim_j:(g + 1) * dim_j, :], picked)
            start = pl.multiple_of((t * 9 + w) * dim_j, 16)
            out[pl.ds(start, dim_j), :] = picked + bias[t]
        return carry

    lax.fori_loop(0, 9, one, 0)
    used = 18 * dim_j
    if out.shape[0] > used:
        out[used:, :] = jnp.zeros((out.shape[0] - used, slots), jnp.float32)


def evidence_kernel(dom, rotations, used, part, meta, like, stat, landed, s0, r0, s1, r1, s2, r2):
    d = lax.axis_index("dom")
    greet(dom, 0)

    def to(k):
        return lax.rem(d + k, dom)

    def scatter(k):
        return remote(part.at[to(k)], landed.at[d], s0.at[k], r0.at[k], {"dom": to(k)})

    def spread_like(k):
        return remote(like.at[d], like.at[d], s1.at[k], r1.at[k], {"dom": to(k)})

    def spread_stat(k):
        return remote(stat.at[d], stat.at[d], s2.at[k], r2.at[k], {"dom": to(k)})

    def start(k, carry):
        scatter(k).start()
        return carry

    lax.fori_loop(1, dom, start, 0)

    def take(k, carry):
        scatter(k).wait_recv()
        return carry + landed[lax.rem(d + dom - k, dom)]

    total = lax.fori_loop(1, dom, take, part[d])
    row = lax.broadcasted_iota(jnp.int32, total.shape, 0)
    prior = jnp.broadcast_to(meta[2:3, :], total.shape)
    delta = jnp.abs(row % rotations - prior)
    dist = jnp.minimum(delta, rotations - delta).astype(jnp.float32)
    valid = row + d * total.shape[0] < used
    loglik = jnp.where(valid, total - LAMBDA * dist * dist, NEG_BIG)
    top = jnp.max(loglik, axis=0, keepdims=True)
    value = jnp.where(valid, jnp.exp(loglik - top), 0.0)
    like[d] = value.astype(jnp.bfloat16)
    mass = jnp.sum(value, axis=0, keepdims=True)
    pick = lax.broadcasted_iota(jnp.int32, stat.shape[1:], 0)
    stat[d] = jnp.where(pick == 0, top, mass)

    def give(k, carry):
        scatter(k).wait_send()
        spread_like(k).start()
        spread_stat(k).start()
        return carry

    lax.fori_loop(1, dom, give, 0)

    def finish(k, carry):
        spread_like(k).wait()
        spread_stat(k).wait()
        return carry

    lax.fori_loop(1, dom, finish, 0)


def sums_kernel(groups, dim_j, like, stat, meta, shifted, out, evidence, post, dense, acc):
    dom, rows, slots = like.shape
    top = stat[:, 0, :]
    mass = stat[:, 1, :]
    peak = jnp.max(top, axis=0, keepdims=True)
    total = jnp.sum(mass * jnp.exp(top - peak), axis=0, keepdims=True)
    ev = peak + jnp.log(total)
    evidence[...] = jnp.broadcast_to(ev, evidence.shape)

    def scale(k, carry):
        factor = jnp.exp(stat[k, 0:1, :] - ev)
        post[pl.ds(pl.multiple_of(k * rows, 16), rows), :] = (like[k].astype(jnp.float32) * factor).astype(jnp.bfloat16)
        return carry

    lax.fori_loop(0, dom, scale, 0)
    names = [jnp.broadcast_to(meta[t:t + 1, :], (dim_j, slots)) for t in range(2)]

    def one(w, carry):
        p0 = post[pl.ds(pl.multiple_of(w * dim_j, 16), dim_j), :].astype(jnp.float32)
        p1 = post[pl.ds(pl.multiple_of((9 + w) * dim_j, 16), dim_j), :].astype(jnp.float32)
        for g in range(groups):
            weight = jnp.where(names[0] == g, p0, jnp.where(names[1] == g, p1, 0.0))
            dense[g * dim_j:(g + 1) * dim_j, :] = weight.astype(jnp.bfloat16)
        acc[...] += jnp.dot(dense[...], shifted[w], preferred_element_type=jnp.float32)
        return carry

    acc[...] = jnp.zeros_like(acc)
    lax.fori_loop(0, 9, one, 0)
    out[...] = acc[...].astype(jnp.bfloat16)


def collect_kernel(ring, part, out, from_left, from_right, rs, rr, ls, lr):
    z = lax.axis_index("cls")
    right, left = lax.rem(z + 1, ring), lax.rem(z + ring - 1, ring)
    greet(0, ring)
    parts = chunks(part.shape[1])
    steps_r = ring // 2
    steps_l = ring - 1 - steps_r
    sent = {}
    for step in range(steps_r):
        for c, (first, size) in enumerate(parts):
            cut = pl.ds(first, size)
            for to_right in (True, False):
                if step >= (steps_r if to_right else steps_l):
                    continue
                hold = from_left if to_right else from_right
                owner = lax.rem(z + steps_r - step, ring) if to_right else lax.rem(z + ring - steps_l + step, ring)
                src = part.at[owner, cut]
                if step:
                    sent[step - 1, c, to_right].wait_recv()
                    hold[step - 1, cut] = (
                        hold[step - 1, cut].astype(jnp.float32) + part[owner, cut].astype(jnp.float32)
                    ).astype(jnp.bfloat16)
                    src = hold.at[step - 1, cut]
                send, recv = (rs, rr) if to_right else (ls, lr)
                copy = remote(
                    src, hold.at[step, cut], send.at[step, c], recv.at[step, c],
                    {"cls": right if to_right else left},
                )
                copy.start()
                sent[step, c, to_right] = copy
    for c, (first, size) in enumerate(parts):
        cut = pl.ds(first, size)
        sent[steps_r - 1, c, True].wait_recv()
        sent[steps_l - 1, c, False].wait_recv()
        out[cut] = (
            part[z, cut].astype(jnp.float32)
            + from_left[steps_r - 1, cut].astype(jnp.float32)
            + from_right[steps_l - 1, cut].astype(jnp.float32)
        )
    for copy in sent.values():
        copy.wait_send()


def per_device(particles, centers, rot_prior, groups, references):
    count, height, width = particles.shape
    dom = lax.axis_size("dom")
    ring = lax.axis_size("cls")
    rotations = references.shape[1]
    dim_j = references.shape[0] * rotations
    own_rows = height // dom
    pixels = own_rows * width
    strip = own_rows + 2
    slots = dom * count
    sem = pltpu.SemaphoreType.DMA

    line = jnp.arange(dom * strip, dtype=jnp.int32)
    line = (line // strip) * own_rows + line % strip - 1
    inside = (line >= 0) & (line < height)
    rows = jnp.arange(height, dtype=jnp.int32)
    cols = jnp.arange(width, dtype=jnp.int32)
    row_sel = (
        (rows[None, None, :] == line[None, :, None] + centers[:, 0, None, None]) & inside[None, :, None]
    ).astype(jnp.bfloat16)
    col_sel = (cols[None, None, :] == cols[None, :, None] + centers[:, 1, None, None]).astype(jnp.bfloat16)
    moved = jnp.einsum("kua,kav->kuv", row_sel, particles, preferred_element_type=jnp.float32).astype(jnp.bfloat16)
    strips = jnp.einsum("kub,kvb->kuv", moved, col_sel, preferred_element_type=jnp.float32).astype(jnp.bfloat16)
    strips = strips.reshape(count, dom, strip, width).transpose(1, 2, 0, 3)
    notes = jnp.concatenate([groups, rot_prior[:, None]], axis=1).astype(jnp.bfloat16)
    notes = jnp.pad(notes, ((0, 0), (0, width - notes.shape[1])))
    strips = jnp.concatenate([strips, jnp.broadcast_to(notes, (dom, 1, count, width))], axis=1)

    refs = references.reshape(dim_j // 16, 16, pixels)
    all_refs, all_strips = spread(dom, ring, refs, strips)
    meta = all_strips[:, strip].reshape(slots, width)[:, :8].T.astype(jnp.int32)

    share = -(-18 * dim_j // (16 * dom)) * 16
    shifted, part = pl.pallas_call(
        functools.partial(score_kernel, ring, dim_j),
        out_shape=(
            jax.ShapeDtypeStruct((9, slots, pixels), jnp.bfloat16),
            jax.ShapeDtypeStruct((dom * share, slots), jnp.float32),
        ),
        in_specs=[VMEM] * 3,
        out_specs=(VMEM, VMEM),
        scratch_shapes=[
            pltpu.VMEM((ring * dim_j, slots), jnp.float32),
            pltpu.VMEM((2, dim_j, slots), jnp.float32),
        ],
    )(all_refs.reshape(ring * dim_j, pixels), all_strips, meta)

    like, stat = pl.pallas_call(
        functools.partial(evidence_kernel, dom, rotations, 18 * dim_j),
        out_shape=(
            jax.ShapeDtypeStruct((dom, share, slots), jnp.bfloat16),
            jax.ShapeDtypeStruct((dom, 8, slots), jnp.float32),
        ),
        in_specs=[VMEM] * 2,
        out_specs=(VMEM, VMEM),
        scratch_shapes=[pltpu.VMEM((dom, share, slots), jnp.float32)] + [sem((dom,))] * 6,
        compiler_params=pltpu.CompilerParams(collective_id=1, has_side_effects=True),
    )(part.reshape(dom, share, slots), meta)

    sums, evidence = pl.pallas_call(
        functools.partial(sums_kernel, ring, dim_j),
        out_shape=(
            jax.ShapeDtypeStruct((ring * dim_j, pixels), jnp.bfloat16),
            jax.ShapeDtypeStruct((8, slots), jnp.float32),
        ),
        in_specs=[VMEM] * 4,
        out_specs=(VMEM, VMEM),
        scratch_shapes=[
            pltpu.VMEM((dom * share, slots), jnp.bfloat16),
            pltpu.VMEM((ring * dim_j, slots), jnp.bfloat16),
            pltpu.VMEM((ring * dim_j, pixels), jnp.float32),
        ],
    )(like, stat, meta, shifted)

    half = ring // 2
    block = (dim_j // 16, 16, pixels)
    total = pl.pallas_call(
        functools.partial(collect_kernel, ring),
        out_shape=jax.ShapeDtypeStruct(block, jnp.float32),
        in_specs=[VMEM],
        out_specs=VMEM,
        scratch_shapes=[pltpu.VMEM((half,) + block, jnp.bfloat16)] * 2 + [sem((half, 2))] * 4,
        compiler_params=pltpu.CompilerParams(collective_id=2, has_side_effects=True),
    )(sums.reshape((ring,) + block))
    class_sums = total.reshape(references.shape[0], rotations, pixels).transpose(2, 0, 1)
    log_evidence = lax.dynamic_slice(evidence[0], (lax.axis_index("dom") * count,), (count,))
    return class_sums, log_evidence


def solution(mesh):
    placed = (
        P(("dom", "cls"), None, None),
        P(("dom", "cls"), None),
        P(("dom", "cls")),
        P(("dom", "cls"), None),
        P("cls", None, "dom"),
    )
    return jax.shard_map(
        per_device,
        mesh=mesh,
        in_specs=placed,
        out_specs=(P("dom", "cls", None), P(("dom", "cls"))),
        check_vma=False,
    )
```

```python
import functools

import jax
import jax.numpy as jnp
from jax import lax
from jax.experimental import pallas as pl
from jax.experimental.pallas import tpu as pltpu
from jax.sharding import PartitionSpec as P

LAMBDA = 1.0
NEG_BIG = -1e30
LANES = 128
VMEM = pl.BlockSpec(memory_space=pltpu.VMEM)
MESH = pl.DeviceIdType.MESH


def remote(src, dst, send_sem, recv_sem, peer):
    return pltpu.make_async_remote_copy(
        src_ref=src, dst_ref=dst, send_sem=send_sem, recv_sem=recv_sem, device_id=peer, device_id_type=MESH
    )


def signal_all(peers, ring):
    barrier = pltpu.get_barrier_semaphore()
    total = 0
    if peers is not None:
        first, last, name = peers

        def one(k, carry):
            pl.semaphore_signal(barrier, inc=1, device_id={"dom": name(k)}, device_id_type=MESH)
            return carry

        lax.fori_loop(first, last, one, 0)
        total += last - first
    if ring:
        z = lax.axis_index("cls")
        for step in (1, ring - 1):
            pl.semaphore_signal(barrier, inc=1, device_id={"cls": lax.rem(z + step, ring)}, device_id_type=MESH)
        total += 2
    return barrier, total


def greet(peers, ring):
    barrier, total = signal_all(peers, ring)
    pl.semaphore_wait(barrier, total)


def chunks(blocks):
    return [(c, 1) for c in range(blocks)]


def spread_kernel(dom, ring, refs, imgs, all_refs, all_imgs, rs, rr, ls, lr, ds, dr, local):
    d = lax.axis_index("dom")
    z = lax.axis_index("cls")
    right, left = lax.rem(z + 1, ring), lax.rem(z + ring - 1, ring)
    greet((1, dom, lambda k: lax.rem(d + k, dom)), ring)
    parts = chunks(refs.shape[0])
    steps_r = ring // 2
    steps_l = ring - 1 - steps_r
    own = pltpu.make_async_copy(refs, all_refs.at[z], local.at[0])
    own.start()
    mine = pltpu.make_async_copy(imgs.at[d], all_imgs.at[d], local.at[1])
    mine.start()

    def hop(step, c, to_right):
        first, size = parts[c]
        piece = lax.rem(z + ring - step, ring) if to_right else lax.rem(z + step, ring)
        block = all_refs.at[piece, pl.ds(first, size)]
        src = refs.at[pl.ds(first, size)] if step == 0 else block
        send, recv = (rs, rr) if to_right else (ls, lr)
        return remote(src, block, send.at[step, c], recv.at[step, c], {"cls": right if to_right else left})

    sent = {}
    for c in range(len(parts)):
        for to_right in (True, False):
            sent[0, c, to_right] = hop(0, c, to_right)
            sent[0, c, to_right].start()

    def strip(k):
        peer = lax.rem(d + k, dom)
        return remote(imgs.at[peer], all_imgs.at[d], ds.at[k], dr.at[k], {"dom": peer})

    def start(k, carry):
        strip(k).start()
        return carry

    def finish(k, carry):
        strip(k).wait()
        return carry

    lax.fori_loop(1, dom, start, 0)
    for step in range(1, steps_r):
        for c in range(len(parts)):
            for to_right in (True, False):
                if step < (steps_r if to_right else steps_l):
                    sent[step - 1, c, to_right].wait_recv()
                    sent[step, c, to_right] = hop(step, c, to_right)
                    sent[step, c, to_right].start()
    for c in range(len(parts)):
        sent[steps_r - 1, c, True].wait_recv()
        sent[steps_l - 1, c, False].wait_recv()
    lax.fori_loop(1, dom, finish, 0)
    for copy in sent.values():
        copy.wait_send()
    own.wait()
    mine.wait()


def spread(dom, ring, refs, imgs):
    half = ring // 2
    sem = pltpu.SemaphoreType.DMA
    return pl.pallas_call(
        functools.partial(spread_kernel, dom, ring),
        out_shape=(
            jax.ShapeDtypeStruct((ring,) + refs.shape, refs.dtype),
            jax.ShapeDtypeStruct(imgs.shape, imgs.dtype),
        ),
        in_specs=[VMEM] * 2,
        out_specs=(VMEM, VMEM),
        scratch_shapes=[sem((half, refs.shape[0]))] * 4 + [sem((dom,)), sem((dom,)), sem((2,))],
        compiler_params=pltpu.CompilerParams(collective_id=0, has_side_effects=True),
    )(refs, imgs)


def score_kernel(groups, dim_j, refs, imgs, meta, shifted, out, score, bias):
    dom, strip, count, width = imgs.shape
    own_rows = strip - 3
    slots = dom * count
    lane = lax.broadcasted_iota(jnp.int32, (slots, width), 1)
    for h in range(own_rows + 2):
        mid = imgs[:, h].astype(jnp.float32).reshape(slots, width)
        before = jnp.where(lane == 0, 0.0, pltpu.roll(mid, 1, axis=1))
        after = jnp.where(lane == width - 1, 0.0, pltpu.roll(mid, width - 1, axis=1))
        for sy, plane in enumerate((before, mid, after)):
            plane = plane.astype(jnp.bfloat16)
            for sx in range(3):
                r = h - sx
                if 0 <= r < own_rows:
                    shifted[3 * sx + sy, :, r * width:(r + 1) * width] = plane
    names = [jnp.broadcast_to(meta[t:t + 1, :], (dim_j, slots)) for t in range(2)]

    def add_norm(g, carry):
        rows = pl.ds(pl.multiple_of(g * dim_j, 16), dim_j)
        block = refs[rows, :].astype(jnp.float32)
        norm = jnp.sum(block * block, axis=1, keepdims=True)
        for t in range(2):
            bias[t] = jnp.where(names[t] == g, -0.5 * norm, bias[t])
        return carry

    bias[...] = jnp.zeros_like(bias)
    lax.fori_loop(0, groups, add_norm, 0)

    def one(w, carry):
        score[...] = lax.dot_general(
            refs[...], shifted[w], (((1,), (1,)), ((), ())), preferred_element_type=jnp.float32
        )
        for t in range(2):
            picked = jnp.zeros((dim_j, slots), jnp.float32)
            for g in range(groups):
                picked = jnp.where(names[t] == g, score[g * dim_j:(g + 1) * dim_j, :], picked)
            start = pl.multiple_of((t * 9 + w) * dim_j, 16)
            out[pl.ds(start, dim_j), :] = picked + bias[t]
        return carry

    lax.fori_loop(0, 9, one, 0)
    used = 18 * dim_j
    if out.shape[0] > used:
        out[used:, :] = jnp.zeros((out.shape[0] - used, slots), jnp.float32)


def evidence_kernel(dom, rotations, used, part, meta, like, stat, held, landed, sems):
    d = lax.axis_index("dom")
    core = lax.rem(d, 2)
    chip = d // 2
    chips = dom // 2
    other = chip * 2 + 1 - core

    def at(k):
        return lax.rem(chip + k, chips)

    def back(k):
        return lax.rem(chip + chips - k, chips)

    barrier, total = signal_all((1, chips, lambda k: at(k) * 2 + core), 0)
    pl.semaphore_signal(barrier, inc=1, device_id={"dom": other}, device_id_type=MESH)
    pl.semaphore_wait(barrier, total + 1)

    def swap(k):
        return remote(part.at[at(k) * 2 + 1 - core], held.at[at(k)], sems.at[0, k], sems.at[1, k], {"dom": other})

    def scatter(k):
        return remote(held.at[at(k)], landed.at[chip], sems.at[2, k], sems.at[3, k], {"dom": at(k) * 2 + core})

    def across(ref, first, k):
        return remote(ref.at[d], ref.at[d], sems.at[first, k], sems.at[first + 1, k], {"dom": at(k) * 2 + core})

    def onward(ref, first, k):
        block = ref.at[back(k) * 2 + core]
        return remote(block, block, sems.at[first, k], sems.at[first + 1, k], {"dom": other})

    def each(first, last, fn):
        def body(k, carry):
            fn(k)
            return carry

        lax.fori_loop(first, last, body, 0)

    each(1, chips, lambda k: swap(k).start())
    swap(0).start()

    def merge(k):
        swap(k).wait_recv()
        held[at(k)] += part[at(k) * 2 + core]

    merge(1)

    def step(k):
        merge(k)
        scatter(k - 1).start()

    each(2, chips, step)
    merge(0)
    scatter(chips - 1).start()

    def take(k, carry):
        scatter(k).wait_recv()
        return carry + landed[back(k)]

    total = lax.fori_loop(1, chips, take, held[chip])
    row = lax.broadcasted_iota(jnp.int32, total.shape, 0)
    prior = jnp.broadcast_to(meta[2:3, :], total.shape)
    delta = jnp.abs(row % rotations - prior)
    dist = jnp.minimum(delta, rotations - delta).astype(jnp.float32)
    valid = row + d * total.shape[0] < used
    loglik = jnp.where(valid, total - LAMBDA * dist * dist, NEG_BIG)
    top = jnp.max(loglik, axis=0, keepdims=True)
    value = jnp.where(valid, jnp.exp(loglik - top), 0.0)
    like[d] = value.astype(jnp.bfloat16)
    mass = jnp.sum(value, axis=0, keepdims=True)
    pick = lax.broadcasted_iota(jnp.int32, stat.shape[1:], 0)
    stat[d] = jnp.where(pick == 0, top, mass)
    each(0, chips, lambda k: swap(k).wait_send())

    def give(k):
        scatter(k).wait_send()
        across(like, 4, k).start()
        across(stat, 6, k).start()

    each(1, chips, give)
    onward(like, 8, 0).start()
    onward(stat, 10, 0).start()

    def relay(k):
        across(like, 4, k).wait_recv()
        onward(like, 8, k).start()
        across(stat, 6, k).wait_recv()
        onward(stat, 10, k).start()

    each(1, chips, relay)

    def finish(k):
        onward(like, 8, k).wait()
        onward(stat, 10, k).wait()

    each(0, chips, finish)

    def sent(k):
        across(like, 4, k).wait_send()
        across(stat, 6, k).wait_send()

    each(1, chips, sent)


def sums_kernel(groups, dim_j, like, stat, meta, shifted, out, evidence, post, dense, acc):
    dom, rows, slots = like.shape
    top = stat[:, 0, :]
    mass = stat[:, 1, :]
    peak = jnp.max(top, axis=0, keepdims=True)
    total = jnp.sum(mass * jnp.exp(top - peak), axis=0, keepdims=True)
    ev = peak + jnp.log(total)
    evidence[...] = jnp.broadcast_to(ev, evidence.shape)

    def scale(k, carry):
        factor = jnp.exp(stat[k, 0:1, :] - ev)
        post[pl.ds(pl.multiple_of(k * rows, 16), rows), :] = (like[k].astype(jnp.float32) * factor).astype(jnp.bfloat16)
        return carry

    lax.fori_loop(0, dom, scale, 0)
    names = [jnp.broadcast_to(meta[t:t + 1, :], (dim_j, slots)) for t in range(2)]

    def one(w, carry):
        p0 = post[pl.ds(pl.multiple_of(w * dim_j, 16), dim_j), :].astype(jnp.float32)
        p1 = post[pl.ds(pl.multiple_of((9 + w) * dim_j, 16), dim_j), :].astype(jnp.float32)
        for g in range(groups):
            weight = jnp.where(names[0] == g, p0, jnp.where(names[1] == g, p1, 0.0))
            dense[g * dim_j:(g + 1) * dim_j, :] = weight.astype(jnp.bfloat16)
        acc[...] += jnp.dot(dense[...], shifted[w], preferred_element_type=jnp.float32)
        return carry

    acc[...] = jnp.zeros_like(acc)
    lax.fori_loop(0, 9, one, 0)
    out[...] = acc[...].astype(jnp.bfloat16)


def collect_kernel(ring, part, out, from_left, from_right, rs, rr, ls, lr):
    z = lax.axis_index("cls")
    right, left = lax.rem(z + 1, ring), lax.rem(z + ring - 1, ring)
    greet(None, ring)
    parts = chunks(part.shape[1])
    steps_r = ring // 2
    steps_l = ring - 1 - steps_r
    sent = {}
    for step in range(steps_r):
        for c, (first, size) in enumerate(parts):
            cut = pl.ds(first, size)
            for to_right in (True, False):
                if step >= (steps_r if to_right else steps_l):
                    continue
                hold = from_left if to_right else from_right
                owner = lax.rem(z + steps_r - step, ring) if to_right else lax.rem(z + ring - steps_l + step, ring)
                src = part.at[owner, cut]
                if step:
                    sent[step - 1, c, to_right].wait_recv()
                    hold[step - 1, cut] = (
                        hold[step - 1, cut].astype(jnp.float32) + part[owner, cut].astype(jnp.float32)
                    ).astype(jnp.bfloat16)
                    src = hold.at[step - 1, cut]
                send, recv = (rs, rr) if to_right else (ls, lr)
                copy = remote(
                    src, hold.at[step, cut], send.at[step, c], recv.at[step, c],
                    {"cls": right if to_right else left},
                )
                copy.start()
                sent[step, c, to_right] = copy
    for c, (first, size) in enumerate(parts):
        cut = pl.ds(first, size)
        sent[steps_r - 1, c, True].wait_recv()
        sent[steps_l - 1, c, False].wait_recv()
        out[cut] = (
            part[z, cut].astype(jnp.float32)
            + from_left[steps_r - 1, cut].astype(jnp.float32)
            + from_right[steps_l - 1, cut].astype(jnp.float32)
        )
    for copy in sent.values():
        copy.wait_send()


def per_device(particles, centers, rot_prior, groups, references):
    count, height, width = particles.shape
    dom = lax.axis_size("dom")
    ring = lax.axis_size("cls")
    rotations = references.shape[1]
    dim_j = references.shape[0] * rotations
    own_rows = height // dom
    pixels = own_rows * width
    strip = own_rows + 2
    slots = dom * count
    sem = pltpu.SemaphoreType.DMA

    line = jnp.arange(dom * strip, dtype=jnp.int32)
    line = (line // strip) * own_rows + line % strip - 1
    inside = (line >= 0) & (line < height)
    rows = jnp.arange(height, dtype=jnp.int32)
    cols = jnp.arange(width, dtype=jnp.int32)
    row_sel = (
        (rows[None, None, :] == line[None, :, None] + centers[:, 0, None, None]) & inside[None, :, None]
    ).astype(jnp.bfloat16)
    col_sel = (cols[None, None, :] == cols[None, :, None] + centers[:, 1, None, None]).astype(jnp.bfloat16)
    moved = jnp.einsum("kua,kav->kuv", row_sel, particles, preferred_element_type=jnp.float32).astype(jnp.bfloat16)
    strips = jnp.einsum("kub,kvb->kuv", moved, col_sel, preferred_element_type=jnp.float32).astype(jnp.bfloat16)
    strips = strips.reshape(count, dom, strip, width).transpose(1, 2, 0, 3)
    notes = jnp.concatenate([groups, rot_prior[:, None]], axis=1).astype(jnp.bfloat16)
    notes = jnp.pad(notes, ((0, 0), (0, width - notes.shape[1])))
    strips = jnp.concatenate([strips, jnp.broadcast_to(notes, (dom, 1, count, width))], axis=1)

    refs = references.reshape(dim_j // 16, 16, pixels)
    all_refs, all_strips = spread(dom, ring, refs, strips)
    meta = all_strips[:, strip].reshape(slots, width)[:, :8].T.astype(jnp.int32)

    share = -(-18 * dim_j // (16 * dom)) * 16
    shifted, part = pl.pallas_call(
        functools.partial(score_kernel, ring, dim_j),
        out_shape=(
            jax.ShapeDtypeStruct((9, slots, pixels), jnp.bfloat16),
            jax.ShapeDtypeStruct((dom * share, slots), jnp.float32),
        ),
        in_specs=[VMEM] * 3,
        out_specs=(VMEM, VMEM),
        scratch_shapes=[
            pltpu.VMEM((ring * dim_j, slots), jnp.float32),
            pltpu.VMEM((2, dim_j, slots), jnp.float32),
        ],
    )(all_refs.reshape(ring * dim_j, pixels), all_strips, meta)

    like, stat = pl.pallas_call(
        functools.partial(evidence_kernel, dom, rotations, 18 * dim_j),
        out_shape=(
            jax.ShapeDtypeStruct((dom, share, slots), jnp.bfloat16),
            jax.ShapeDtypeStruct((dom, 2, slots), jnp.float32),
        ),
        in_specs=[VMEM] * 2,
        out_specs=(VMEM, VMEM),
        scratch_shapes=[pltpu.VMEM((dom // 2, share, slots), jnp.float32)] * 2 + [sem((12, dom // 2))],
        compiler_params=pltpu.CompilerParams(collective_id=1, has_side_effects=True),
    )(part.reshape(dom, share, slots), meta)

    sums, evidence = pl.pallas_call(
        functools.partial(sums_kernel, ring, dim_j),
        out_shape=(
            jax.ShapeDtypeStruct((ring * dim_j, pixels), jnp.bfloat16),
            jax.ShapeDtypeStruct((8, slots), jnp.float32),
        ),
        in_specs=[VMEM] * 4,
        out_specs=(VMEM, VMEM),
        scratch_shapes=[
            pltpu.VMEM((dom * share, slots), jnp.bfloat16),
            pltpu.VMEM((ring * dim_j, slots), jnp.bfloat16),
            pltpu.VMEM((ring * dim_j, pixels), jnp.float32),
        ],
    )(like, stat, meta, shifted)

    half = ring // 2
    block = (dim_j // 16, 16, pixels)
    total = pl.pallas_call(
        functools.partial(collect_kernel, ring),
        out_shape=jax.ShapeDtypeStruct(block, jnp.float32),
        in_specs=[VMEM],
        out_specs=VMEM,
        scratch_shapes=[pltpu.VMEM((half,) + block, jnp.bfloat16)] * 2 + [sem((half, block[0]))] * 4,
        compiler_params=pltpu.CompilerParams(collective_id=2, has_side_effects=True),
    )(sums.reshape((ring,) + block))
    class_sums = total.reshape(references.shape[0], rotations, pixels).transpose(2, 0, 1)
    log_evidence = lax.dynamic_slice(evidence[0], (lax.axis_index("dom") * count,), (count,))
    return class_sums, log_evidence


def solution(mesh):
    placed = (
        P(("dom", "cls"), None, None),
        P(("dom", "cls"), None),
        P(("dom", "cls")),
        P(("dom", "cls"), None),
        P("cls", None, "dom"),
    )
    return jax.shard_map(
        per_device,
        mesh=mesh,
        in_specs=placed,
        out_specs=(P("dom", "cls", None), P(("dom", "cls"))),
        check_vma=False,
    )
```

```python
import functools

import jax
import jax.numpy as jnp
from jax import lax
from jax.experimental import pallas as pl
from jax.experimental.pallas import tpu as pltpu
from jax.sharding import PartitionSpec as P

LAMBDA = 1.0
NEG_BIG = -1e30
LANES = 128
VMEM = pl.BlockSpec(memory_space=pltpu.VMEM)
MESH = pl.DeviceIdType.MESH


def remote(src, dst, send_sem, recv_sem, peer):
    return pltpu.make_async_remote_copy(
        src_ref=src, dst_ref=dst, send_sem=send_sem, recv_sem=recv_sem, device_id=peer, device_id_type=MESH
    )


def signal_all(peers, ring):
    barrier = pltpu.get_barrier_semaphore()
    total = 0
    if peers is not None:
        first, last, name = peers

        def one(k, carry):
            pl.semaphore_signal(barrier, inc=1, device_id={"dom": name(k)}, device_id_type=MESH)
            return carry

        lax.fori_loop(first, last, one, 0)
        total += last - first
    if ring:
        z = lax.axis_index("cls")
        for step in (1, ring - 1):
            pl.semaphore_signal(barrier, inc=1, device_id={"cls": lax.rem(z + step, ring)}, device_id_type=MESH)
        total += 2
    return barrier, total


def greet(peers, ring):
    barrier, total = signal_all(peers, ring)
    pl.semaphore_wait(barrier, total)


def chunks(blocks):
    return [(c, 1) for c in range(blocks)]


def each(first, last, fn):
    def body(k, carry):
        fn(k)
        return carry

    lax.fori_loop(first, last, body, 0)


def score_kernel(dom, ring, refs, imgs, shifted, out, meta, all_refs, all_imgs, score, rs, rr, ls, lr, ds, dr, local):
    d = lax.axis_index("dom")
    z = lax.axis_index("cls")
    right, left = lax.rem(z + 1, ring), lax.rem(z + ring - 1, ring)
    blocks, sixteen, pixels = refs.shape
    dim_j = blocks * sixteen
    strip, count, width = imgs.shape[1:]
    own_rows = strip - 3
    slots = dom * count
    steps_r = ring // 2
    steps_l = ring - 1 - steps_r
    greet((1, dom, lambda k: lax.rem(d + k, dom)), ring)
    own = pltpu.make_async_copy(refs, all_refs.at[z], local.at[0])
    own.start()
    mine = pltpu.make_async_copy(imgs.at[d], all_imgs.at[d], local.at[1])
    mine.start()

    def hop(step, c, to_right, src=None):
        piece = lax.rem(z + ring - step, ring) if to_right else lax.rem(z + step, ring)
        block = all_refs.at[piece, c]
        send, recv = (rs, rr) if to_right else (ls, lr)
        return remote(
            block if src is None else src, block, send.at[step, c], recv.at[step, c],
            {"cls": right if to_right else left},
        )

    for c in range(blocks):
        for to_right in (True, False):
            hop(0, c, to_right, refs.at[c]).start()

    def sent_strip(k):
        peer = lax.rem(d + k, dom)
        return remote(imgs.at[peer], all_imgs.at[d], ds.at[k], dr.at[k], {"dom": peer})

    each(1, dom, lambda k: sent_strip(k).start())
    out[...] = jnp.zeros_like(out)
    each(1, dom, lambda k: sent_strip(k).wait())
    mine.wait()
    own.wait()

    def forward(step, to_left):
        for c in range(blocks):
            hop(step - 1, c, True).wait_recv()
            hop(step, c, True).start()
            hop(step - 1, c, False).wait_recv()
            if to_left:
                hop(step, c, False).start()

    forward(1, True)
    lane = lax.broadcasted_iota(jnp.int32, (slots, width), 1)
    for h in range(own_rows + 2):
        mid = all_imgs[:, h].astype(jnp.float32).reshape(slots, width)
        before = jnp.where(lane == 0, 0.0, pltpu.roll(mid, 1, axis=1))
        after = jnp.where(lane == width - 1, 0.0, pltpu.roll(mid, width - 1, axis=1))
        for sy, plane in enumerate((before, mid, after)):
            plane = plane.astype(jnp.bfloat16)
            for sx in range(3):
                r = h - sx
                if 0 <= r < own_rows:
                    first = (3 * sx + sy) * slots
                    shifted[first:first + slots, r * width:(r + 1) * width] = plane
    notes = all_imgs[:, strip - 1].astype(jnp.float32).reshape(slots, width)
    meta[...] = jnp.transpose(notes)[:8].astype(jnp.int32)
    names = [jnp.broadcast_to(meta[t:t + 1, :], (dim_j, slots)) for t in range(2)]

    def pair(ga, gb):
        both = jnp.concatenate(
            [all_refs[ga].reshape(dim_j, pixels), all_refs[gb].reshape(dim_j, pixels)], axis=0
        )
        score[...] = lax.dot_general(
            both, shifted[...], (((1,), (1,)), ((), ())), preferred_element_type=jnp.float32
        )
        wide = both.astype(jnp.float32)
        bias = -0.5 * jnp.sum(wide * wide, axis=1, keepdims=True)

        def pick(w):
            cols = pl.ds(pl.multiple_of(w * slots, LANES), slots)
            first = score[0:dim_j, cols] + bias[:dim_j]
            second = score[dim_j:, cols] + bias[dim_j:]
            for t in range(2):
                rows = pl.ds(pl.multiple_of((t * 9 + w) * dim_j, 16), dim_j)
                out[rows, :] = jnp.where(
                    names[t] == ga, first, jnp.where(names[t] == gb, second, out[rows, :])
                )

        each(0, 9, pick)

    def near(step):
        pair(lax.rem(z + ring - step, ring), lax.rem(z + step, ring))

    near(1)

    def middle(step):
        forward(step, True)
        near(step)

    each(2, steps_l, middle)
    forward(steps_l, False)
    near(steps_l)
    for c in range(blocks):
        hop(steps_r - 1, c, True).wait_recv()
    pair(lax.rem(z + steps_r, ring), z)

    def drain(step):
        for c in range(blocks):
            hop(step, c, True).wait_send()

    def drain_left(step):
        for c in range(blocks):
            hop(step, c, False).wait_send()

    each(0, steps_r, drain)
    each(0, steps_l, drain_left)


def evidence_kernel(dom, rotations, used, part, meta, like, stat, held, landed, sems):
    d = lax.axis_index("dom")
    core = lax.rem(d, 2)
    chip = d // 2
    chips = dom // 2
    other = chip * 2 + 1 - core

    def at(k):
        return lax.rem(chip + k, chips)

    def back(k):
        return lax.rem(chip + chips - k, chips)

    barrier, total = signal_all((1, chips, lambda k: at(k) * 2 + core), 0)
    pl.semaphore_signal(barrier, inc=1, device_id={"dom": other}, device_id_type=MESH)
    pl.semaphore_wait(barrier, total + 1)

    def swap(k):
        return remote(part.at[at(k) * 2 + 1 - core], held.at[at(k)], sems.at[0, k], sems.at[1, k], {"dom": other})

    def scatter(k):
        return remote(held.at[at(k)], landed.at[chip], sems.at[2, k], sems.at[3, k], {"dom": at(k) * 2 + core})

    def across(ref, first, k):
        return remote(ref.at[d], ref.at[d], sems.at[first, k], sems.at[first + 1, k], {"dom": at(k) * 2 + core})

    def onward(ref, first, k):
        block = ref.at[back(k) * 2 + core]
        return remote(block, block, sems.at[first, k], sems.at[first + 1, k], {"dom": other})

    each(1, chips, lambda k: swap(k).start())
    swap(0).start()

    def merge(k):
        swap(k).wait_recv()
        held[at(k)] += part[at(k) * 2 + core]

    merge(1)

    def step(k):
        merge(k)
        scatter(k - 1).start()

    each(2, chips, step)
    merge(0)
    scatter(chips - 1).start()

    def take(k, carry):
        scatter(k).wait_recv()
        return carry + landed[back(k)]

    total = lax.fori_loop(1, chips, take, held[chip])
    row = lax.broadcasted_iota(jnp.int32, total.shape, 0)
    prior = jnp.broadcast_to(meta[2:3, :], total.shape)
    delta = jnp.abs(row % rotations - prior)
    dist = jnp.minimum(delta, rotations - delta).astype(jnp.float32)
    valid = row + d * total.shape[0] < used
    loglik = jnp.where(valid, total - LAMBDA * dist * dist, NEG_BIG)
    top = jnp.max(loglik, axis=0, keepdims=True)
    value = jnp.where(valid, jnp.exp(loglik - top), 0.0)
    like[d] = value.astype(jnp.bfloat16)
    mass = jnp.sum(value, axis=0, keepdims=True)
    pick = lax.broadcasted_iota(jnp.int32, stat.shape[1:], 0)
    stat[d] = jnp.where(pick == 0, top, mass)
    each(0, chips, lambda k: swap(k).wait_send())

    def give(k):
        scatter(k).wait_send()
        across(like, 4, k).start()
        across(stat, 6, k).start()

    each(1, chips, give)
    onward(like, 8, 0).start()
    onward(stat, 10, 0).start()

    def relay(k):
        across(like, 4, k).wait_recv()
        onward(like, 8, k).start()
        across(stat, 6, k).wait_recv()
        onward(stat, 10, k).start()

    each(1, chips, relay)

    def finish(k):
        onward(like, 8, k).wait()
        onward(stat, 10, k).wait()

    each(0, chips, finish)

    def sent(k):
        across(like, 4, k).wait_send()
        across(stat, 6, k).wait_send()

    each(1, chips, sent)


def sums_kernel(ring, like, stat, meta, shifted, out, evidence, post, dense, part, from_left, from_right, rs, rr, ls, lr):
    z = lax.axis_index("cls")
    right, left = lax.rem(z + 1, ring), lax.rem(z + ring - 1, ring)
    barrier, greetings = signal_all(None, ring)
    dom, rows, slots = like.shape
    blocks, sixteen, pixels = out.shape
    dim_j = blocks * sixteen
    steps_r = ring // 2
    steps_l = ring - 1 - steps_r
    top = stat[:, 0, :]
    mass = stat[:, 1, :]
    peak = jnp.max(top, axis=0, keepdims=True)
    total = jnp.sum(mass * jnp.exp(top - peak), axis=0, keepdims=True)
    ev = peak + jnp.log(total)
    evidence[...] = jnp.broadcast_to(ev, evidence.shape)

    def scale(k):
        factor = jnp.exp(stat[k, 0:1, :] - ev)
        post[pl.ds(pl.multiple_of(k * rows, 16), rows), :] = (like[k].astype(jnp.float32) * factor).astype(jnp.bfloat16)

    each(0, dom, scale)
    names = [jnp.broadcast_to(meta[t:t + 1, :], (dim_j, slots)) for t in range(2)]

    def pair(ga, gb):
        for w in range(9):
            p0 = post[w * dim_j:(w + 1) * dim_j, :].astype(jnp.float32)
            p1 = post[(9 + w) * dim_j:(10 + w) * dim_j, :].astype(jnp.float32)
            for first, g in ((0, ga), (dim_j, gb)):
                weight = jnp.where(names[0] == g, p0, jnp.where(names[1] == g, p1, 0.0))
                dense[first:first + dim_j, w * slots:(w + 1) * slots] = weight.astype(jnp.bfloat16)
        sums = jnp.dot(dense[...], shifted[...], preferred_element_type=jnp.float32).astype(jnp.bfloat16)
        part[ga] = sums[:dim_j].reshape(blocks, sixteen, pixels)
        part[gb] = sums[dim_j:].reshape(blocks, sixteen, pixels)

    def hop(step, c, to_right, src=None):
        hold, send, recv = (from_left, rs, rr) if to_right else (from_right, ls, lr)
        return remote(
            hold.at[step - 1, c] if src is None else src, hold.at[step, c], send.at[step, c], recv.at[step, c],
            {"cls": right if to_right else left},
        )

    def add_on(step, c, to_right, owner):
        hold = from_left if to_right else from_right
        hop(step - 1, c, to_right, part.at[owner, c]).wait_recv()
        hold[step - 1, c] = (
            hold[step - 1, c].astype(jnp.float32) + part[owner, c].astype(jnp.float32)
        ).astype(jnp.bfloat16)
        hop(step, c, to_right).start()

    far = lax.rem(z + steps_r, ring)
    pair(far, z)
    pl.semaphore_wait(barrier, greetings)
    for c in range(blocks):
        hop(0, c, True, part.at[far, c]).start()

    def owners(i):
        return lax.rem(z + steps_l - i, ring), lax.rem(z + ring - steps_l + i, ring)

    first_r, first_l = owners(0)
    pair(first_r, first_l)
    for c in range(blocks):
        hop(0, c, False, part.at[first_l, c]).start()
    for c in range(blocks):
        add_on(1, c, True, first_r)

    def step(i):
        owner_r, owner_l = owners(i)
        pair(owner_r, owner_l)
        for c in range(blocks):
            add_on(i, c, False, owner_l)
            add_on(i + 1, c, True, owner_r)

    each(1, steps_l, step)
    for c in range(blocks):
        hop(steps_r - 1, c, True).wait_recv()
        hop(steps_l - 1, c, False).wait_recv()
        out[c] = (
            part[z, c].astype(jnp.float32)
            + from_left[steps_r - 1, c].astype(jnp.float32)
            + from_right[steps_l - 1, c].astype(jnp.float32)
        )
    for to_right, steps in ((True, steps_r), (False, steps_l)):
        for c in range(blocks):
            hop(0, c, to_right, part.at[z, c]).wait_send()

        def drain(i):
            for c in range(blocks):
                hop(i, c, to_right).wait_send()

        each(1, steps, drain)


def per_device(particles, centers, rot_prior, groups, references):
    count, height, width = particles.shape
    dom = lax.axis_size("dom")
    ring = lax.axis_size("cls")
    rotations = references.shape[1]
    dim_j = references.shape[0] * rotations
    own_rows = height // dom
    pixels = own_rows * width
    strip = own_rows + 2
    slots = dom * count
    sem = pltpu.SemaphoreType.DMA

    line = jnp.arange(dom * strip, dtype=jnp.int32)
    line = (line // strip) * own_rows + line % strip - 1
    inside = (line >= 0) & (line < height)
    rows = jnp.arange(height, dtype=jnp.int32)
    cols = jnp.arange(width, dtype=jnp.int32)
    row_sel = (
        (rows[None, None, :] == line[None, :, None] + centers[:, 0, None, None]) & inside[None, :, None]
    ).astype(jnp.bfloat16)
    col_sel = (cols[None, None, :] == cols[None, :, None] + centers[:, 1, None, None]).astype(jnp.bfloat16)
    moved = jnp.einsum("kua,kav->kuv", row_sel, particles, preferred_element_type=jnp.float32).astype(jnp.bfloat16)
    strips = jnp.einsum("kub,kvb->kuv", moved, col_sel, preferred_element_type=jnp.float32).astype(jnp.bfloat16)
    strips = strips.reshape(count, dom, strip, width).transpose(1, 2, 0, 3)
    notes = jnp.concatenate([groups, rot_prior[:, None]], axis=1).astype(jnp.bfloat16)
    notes = jnp.pad(notes, ((0, 0), (0, width - notes.shape[1])))
    strips = jnp.concatenate([strips, jnp.broadcast_to(notes, (dom, 1, count, width))], axis=1)

    refs = references.reshape(dim_j // 16, 16, pixels)
    share = -(-18 * dim_j // (16 * dom)) * 16
    half = ring // 2
    block = refs.shape
    shifted, part, meta = pl.pallas_call(
        functools.partial(score_kernel, dom, ring),
        out_shape=(
            jax.ShapeDtypeStruct((9 * slots, pixels), jnp.bfloat16),
            jax.ShapeDtypeStruct((dom * share, slots), jnp.float32),
            jax.ShapeDtypeStruct((8, slots), jnp.int32),
        ),
        in_specs=[VMEM] * 2,
        out_specs=(VMEM, VMEM, VMEM),
        scratch_shapes=[
            pltpu.VMEM((ring,) + block, jnp.bfloat16),
            pltpu.VMEM(strips.shape, jnp.bfloat16),
            pltpu.VMEM((2 * dim_j, 9 * slots), jnp.float32),
        ]
        + [sem((half, block[0]))] * 4
        + [sem((dom,)), sem((dom,)), sem((2,))],
        compiler_params=pltpu.CompilerParams(collective_id=0, has_side_effects=True),
    )(refs, strips)

    like, stat = pl.pallas_call(
        functools.partial(evidence_kernel, dom, rotations, 18 * dim_j),
        out_shape=(
            jax.ShapeDtypeStruct((dom, share, slots), jnp.bfloat16),
            jax.ShapeDtypeStruct((dom, 2, slots), jnp.float32),
        ),
        in_specs=[VMEM] * 2,
        out_specs=(VMEM, VMEM),
        scratch_shapes=[pltpu.VMEM((dom // 2, share, slots), jnp.float32)] * 2 + [sem((12, dom // 2))],
        compiler_params=pltpu.CompilerParams(collective_id=1, has_side_effects=True),
    )(part.reshape(dom, share, slots), meta)

    total, evidence = pl.pallas_call(
        functools.partial(sums_kernel, ring),
        out_shape=(
            jax.ShapeDtypeStruct(block, jnp.float32),
            jax.ShapeDtypeStruct((8, slots), jnp.float32),
        ),
        in_specs=[VMEM] * 4,
        out_specs=(VMEM, VMEM),
        scratch_shapes=[
            pltpu.VMEM((dom * share, slots), jnp.bfloat16),
            pltpu.VMEM((2 * dim_j, 9 * slots), jnp.bfloat16),
            pltpu.VMEM((ring,) + block, jnp.bfloat16),
        ]
        + [pltpu.VMEM((half,) + block, jnp.bfloat16)] * 2
        + [sem((half, block[0]))] * 4,
        compiler_params=pltpu.CompilerParams(collective_id=2, has_side_effects=True),
    )(like, stat, meta, shifted)
    class_sums = total.reshape(references.shape[0], rotations, pixels).transpose(2, 0, 1)
    log_evidence = lax.dynamic_slice(evidence[0], (lax.axis_index("dom") * count,), (count,))
    return class_sums, log_evidence


def solution(mesh):
    placed = (
        P(("dom", "cls"), None, None),
        P(("dom", "cls"), None),
        P(("dom", "cls")),
        P(("dom", "cls"), None),
        P("cls", None, "dom"),
    )
    return jax.shard_map(
        per_device,
        mesh=mesh,
        in_specs=placed,
        out_specs=(P("dom", "cls", None), P(("dom", "cls"))),
        check_vma=False,
    )
```

```python
import functools

import jax
import jax.numpy as jnp
from jax import lax
from jax.experimental import pallas as pl
from jax.experimental.pallas import tpu as pltpu
from jax.sharding import PartitionSpec as P

LAMBDA = 1.0
NEG_BIG = -1e30
LANES = 128
VMEM = pl.BlockSpec(memory_space=pltpu.VMEM)
MESH = pl.DeviceIdType.MESH


def remote(src, dst, send_sem, recv_sem, peer):
    return pltpu.make_async_remote_copy(
        src_ref=src, dst_ref=dst, send_sem=send_sem, recv_sem=recv_sem, device_id=peer, device_id_type=MESH
    )


def signal_all(peers, ring):
    barrier = pltpu.get_barrier_semaphore()
    total = 0
    if peers is not None:
        first, last, name = peers

        def one(k, carry):
            pl.semaphore_signal(barrier, inc=1, device_id={"dom": name(k)}, device_id_type=MESH)
            return carry

        lax.fori_loop(first, last, one, 0)
        total += last - first
    if ring:
        z = lax.axis_index("cls")
        for step in (1, ring - 1):
            pl.semaphore_signal(barrier, inc=1, device_id={"cls": lax.rem(z + step, ring)}, device_id_type=MESH)
        total += 2
    return barrier, total


def greet(peers, ring):
    barrier, total = signal_all(peers, ring)
    pl.semaphore_wait(barrier, total)


def chunks(blocks):
    return [(c, 1) for c in range(blocks)]


def each(first, last, fn):
    def body(k, carry):
        fn(k)
        return carry

    lax.fori_loop(first, last, body, 0)


def score_kernel(dom, ring, refs, imgs, shifted, out, meta, all_refs, all_imgs, score, rs, rr, ls, lr, ds, dr, local):
    d = lax.axis_index("dom")
    z = lax.axis_index("cls")
    right, left = lax.rem(z + 1, ring), lax.rem(z + ring - 1, ring)
    blocks, sixteen, pixels = refs.shape
    dim_j = blocks * sixteen
    strip, count, width = imgs.shape[1:]
    own_rows = strip - 3
    slots = dom * count
    steps_r = ring // 2
    steps_l = ring - 1 - steps_r
    greet((1, dom, lambda k: lax.rem(d + k, dom)), ring)
    own = pltpu.make_async_copy(refs, all_refs.at[z], local.at[0])
    own.start()
    mine = pltpu.make_async_copy(imgs.at[d], all_imgs.at[d], local.at[1])
    mine.start()

    def hop(step, c, to_right, src=None):
        piece = lax.rem(z + ring - step, ring) if to_right else lax.rem(z + step, ring)
        block = all_refs.at[piece, c]
        send, recv = (rs, rr) if to_right else (ls, lr)
        return remote(
            block if src is None else src, block, send.at[step, c], recv.at[step, c],
            {"cls": right if to_right else left},
        )

    for c in range(blocks):
        for to_right in (True, False):
            hop(0, c, to_right, refs.at[c]).start()

    def sent_strip(k):
        peer = lax.rem(d + k, dom)
        return remote(imgs.at[peer], all_imgs.at[d], ds.at[k], dr.at[k], {"dom": peer})

    each(1, dom, lambda k: sent_strip(k).start())
    out[...] = jnp.zeros_like(out)

    def forward(step, to_left):
        for c in range(blocks):
            hop(step - 1, c, True).wait_recv()
            hop(step, c, True).start()
            hop(step - 1, c, False).wait_recv()
            if to_left:
                hop(step, c, False).start()

    forward(1, True)
    each(1, dom, lambda k: sent_strip(k).wait())
    mine.wait()
    own.wait()
    forward(2, True)
    lane = lax.broadcasted_iota(jnp.int32, (slots, width), 1)
    for h in range(own_rows + 2):
        mid = all_imgs[:, h].astype(jnp.float32).reshape(slots, width)
        before = jnp.where(lane == 0, 0.0, pltpu.roll(mid, 1, axis=1))
        after = jnp.where(lane == width - 1, 0.0, pltpu.roll(mid, width - 1, axis=1))
        for sy, plane in enumerate((before, mid, after)):
            plane = plane.astype(jnp.bfloat16)
            for sx in range(3):
                r = h - sx
                if 0 <= r < own_rows:
                    first = (3 * sx + sy) * slots
                    shifted[first:first + slots, r * width:(r + 1) * width] = plane
    notes = all_imgs[:, strip - 1].astype(jnp.float32).reshape(slots, width)
    meta[...] = jnp.transpose(notes)[:8].astype(jnp.int32)
    names = [jnp.broadcast_to(meta[t:t + 1, :], (dim_j, slots)) for t in range(2)]

    def pair(ga, gb):
        both = jnp.concatenate(
            [all_refs[ga].reshape(dim_j, pixels), all_refs[gb].reshape(dim_j, pixels)], axis=0
        )
        score[...] = lax.dot_general(
            both, shifted[...], (((1,), (1,)), ((), ())), preferred_element_type=jnp.float32
        )
        wide = both.astype(jnp.float32)
        bias = -0.5 * jnp.sum(wide * wide, axis=1, keepdims=True)

        def pick(w):
            cols = pl.ds(pl.multiple_of(w * slots, LANES), slots)
            first = score[0:dim_j, cols] + bias[:dim_j]
            second = score[dim_j:, cols] + bias[dim_j:]
            for t in range(2):
                rows = pl.ds(pl.multiple_of((t * 9 + w) * dim_j, 16), dim_j)
                out[rows, :] = jnp.where(
                    names[t] == ga, first, jnp.where(names[t] == gb, second, out[rows, :])
                )

        each(0, 9, pick)

    def near(step):
        pair(lax.rem(z + ring - step, ring), lax.rem(z + step, ring))

    forward(3, True)
    each(1, 3, near)

    def middle(step):
        forward(step, True)
        near(step - 1)

    each(4, steps_l, middle)
    forward(steps_l, False)
    each(steps_l - 1, steps_l + 1, near)
    for c in range(blocks):
        hop(steps_r - 1, c, True).wait_recv()
    pair(lax.rem(z + steps_r, ring), z)

    def drain(step):
        for c in range(blocks):
            hop(step, c, True).wait_send()

    def drain_left(step):
        for c in range(blocks):
            hop(step, c, False).wait_send()

    each(0, steps_r, drain)
    each(0, steps_l, drain_left)


def evidence_kernel(dom, rotations, used, part, meta, like, stat, held, landed, sems):
    d = lax.axis_index("dom")
    core = lax.rem(d, 2)
    chip = d // 2
    chips = dom // 2
    other = chip * 2 + 1 - core

    def at(k):
        return lax.rem(chip + k, chips)

    def back(k):
        return lax.rem(chip + chips - k, chips)

    barrier, total = signal_all((1, chips, lambda k: at(k) * 2 + core), 0)
    pl.semaphore_signal(barrier, inc=1, device_id={"dom": other}, device_id_type=MESH)
    pl.semaphore_wait(barrier, total + 1)

    def swap(k):
        return remote(part.at[at(k) * 2 + 1 - core], held.at[at(k)], sems.at[0, k], sems.at[1, k], {"dom": other})

    def scatter(k):
        return remote(held.at[at(k)], landed.at[chip], sems.at[2, k], sems.at[3, k], {"dom": at(k) * 2 + core})

    def across(ref, first, k):
        return remote(ref.at[d], ref.at[d], sems.at[first, k], sems.at[first + 1, k], {"dom": at(k) * 2 + core})

    def onward(ref, first, k):
        block = ref.at[back(k) * 2 + core]
        return remote(block, block, sems.at[first, k], sems.at[first + 1, k], {"dom": other})

    each(1, chips, lambda k: swap(k).start())
    swap(0).start()

    def merge(k):
        swap(k).wait_recv()
        held[at(k)] += part[at(k) * 2 + core]

    merge(1)

    def step(k):
        merge(k)
        scatter(k - 1).start()

    each(2, chips, step)
    merge(0)
    scatter(chips - 1).start()

    def take(k, carry):
        scatter(k).wait_recv()
        return carry + landed[back(k)]

    total = lax.fori_loop(1, chips, take, held[chip])
    row = lax.broadcasted_iota(jnp.int32, total.shape, 0)
    prior = jnp.broadcast_to(meta[2:3, :], total.shape)
    delta = jnp.abs(row % rotations - prior)
    dist = jnp.minimum(delta, rotations - delta).astype(jnp.float32)
    valid = row + d * total.shape[0] < used
    loglik = jnp.where(valid, total - LAMBDA * dist * dist, NEG_BIG)
    top = jnp.max(loglik, axis=0, keepdims=True)
    value = jnp.where(valid, jnp.exp(loglik - top), 0.0)
    like[d] = value.astype(jnp.bfloat16)
    mass = jnp.sum(value, axis=0, keepdims=True)
    pick = lax.broadcasted_iota(jnp.int32, stat.shape[1:], 0)
    stat[d] = jnp.where(pick == 0, top, mass)
    each(0, chips, lambda k: swap(k).wait_send())

    def give(k):
        scatter(k).wait_send()
        across(like, 4, k).start()
        across(stat, 6, k).start()

    each(1, chips, give)
    onward(like, 8, 0).start()
    onward(stat, 10, 0).start()

    def relay(k):
        across(like, 4, k).wait_recv()
        onward(like, 8, k).start()
        across(stat, 6, k).wait_recv()
        onward(stat, 10, k).start()

    each(1, chips, relay)

    def finish(k):
        onward(like, 8, k).wait()
        onward(stat, 10, k).wait()

    each(0, chips, finish)

    def sent(k):
        across(like, 4, k).wait_send()
        across(stat, 6, k).wait_send()

    each(1, chips, sent)


def sums_kernel(ring, like, stat, meta, shifted, out, evidence, post, dense, part, from_left, from_right, rs, rr, ls, lr):
    z = lax.axis_index("cls")
    right, left = lax.rem(z + 1, ring), lax.rem(z + ring - 1, ring)
    barrier, greetings = signal_all(None, ring)
    dom, rows, slots = like.shape
    blocks, sixteen, pixels = out.shape
    dim_j = blocks * sixteen
    steps_r = ring // 2
    steps_l = ring - 1 - steps_r
    top = stat[:, 0, :]
    mass = stat[:, 1, :]
    peak = jnp.max(top, axis=0, keepdims=True)
    total = jnp.sum(mass * jnp.exp(top - peak), axis=0, keepdims=True)
    ev = peak + jnp.log(total)
    count = evidence.shape[1]
    turn = lax.rem(slots - lax.axis_index("dom") * count, slots)
    evidence[...] = pltpu.roll(jnp.broadcast_to(ev, (8, slots)), turn, axis=1)[0:1, :count]

    def scale(k):
        factor = jnp.exp(stat[k, 0:1, :] - ev)
        post[pl.ds(pl.multiple_of(k * rows, 16), rows), :] = (like[k].astype(jnp.float32) * factor).astype(jnp.bfloat16)

    each(0, dom, scale)
    names = [jnp.broadcast_to(meta[t:t + 1, :], (dim_j, slots)) for t in range(2)]

    def pair(ga, gb):
        for w in range(9):
            p0 = post[w * dim_j:(w + 1) * dim_j, :].astype(jnp.float32)
            p1 = post[(9 + w) * dim_j:(10 + w) * dim_j, :].astype(jnp.float32)
            for first, g in ((0, ga), (dim_j, gb)):
                weight = jnp.where(names[0] == g, p0, jnp.where(names[1] == g, p1, 0.0))
                dense[first:first + dim_j, w * slots:(w + 1) * slots] = weight.astype(jnp.bfloat16)
        sums = jnp.dot(dense[...], shifted[...], preferred_element_type=jnp.float32).astype(jnp.bfloat16)
        part[ga] = sums[:dim_j].reshape(blocks, sixteen, pixels)
        part[gb] = sums[dim_j:].reshape(blocks, sixteen, pixels)

    def hop(step, c, to_right, src=None):
        hold, send, recv = (from_left, rs, rr) if to_right else (from_right, ls, lr)
        return remote(
            hold.at[step - 1, c] if src is None else src, hold.at[step, c], send.at[step, c], recv.at[step, c],
            {"cls": right if to_right else left},
        )

    def add_on(step, c, to_right, owner):
        hold = from_left if to_right else from_right
        hop(step - 1, c, to_right, part.at[owner, c]).wait_recv()
        hold[step - 1, c] = (
            hold[step - 1, c].astype(jnp.float32) + part[owner, c].astype(jnp.float32)
        ).astype(jnp.bfloat16)
        hop(step, c, to_right).start()

    far = lax.rem(z + steps_r, ring)
    pair(far, z)
    pl.semaphore_wait(barrier, greetings)
    for c in range(blocks):
        hop(0, c, True, part.at[far, c]).start()

    def owners(i):
        return lax.rem(z + steps_l - i, ring), lax.rem(z + ring - steps_l + i, ring)

    first_r, first_l = owners(0)
    pair(first_r, first_l)
    for c in range(blocks):
        hop(0, c, False, part.at[first_l, c]).start()
    for c in range(blocks):
        add_on(1, c, True, first_r)

    def step(i):
        owner_r, owner_l = owners(i)
        pair(owner_r, owner_l)
        for c in range(blocks):
            add_on(i, c, False, owner_l)
            add_on(i + 1, c, True, owner_r)

    each(1, steps_l, step)
    for c in range(blocks):
        hop(steps_r - 1, c, True).wait_recv()
        hop(steps_l - 1, c, False).wait_recv()
        out[c] = (
            part[z, c].astype(jnp.float32)
            + from_left[steps_r - 1, c].astype(jnp.float32)
            + from_right[steps_l - 1, c].astype(jnp.float32)
        )
    for to_right, steps in ((True, steps_r), (False, steps_l)):
        for c in range(blocks):
            hop(0, c, to_right, part.at[z, c]).wait_send()

        def drain(i):
            for c in range(blocks):
                hop(i, c, to_right).wait_send()

        each(1, steps, drain)


def per_device(particles, centers, rot_prior, groups, references):
    count, height, width = particles.shape
    dom = lax.axis_size("dom")
    ring = lax.axis_size("cls")
    rotations = references.shape[1]
    dim_j = references.shape[0] * rotations
    own_rows = height // dom
    pixels = own_rows * width
    strip = own_rows + 2
    slots = dom * count
    sem = pltpu.SemaphoreType.DMA

    line = jnp.arange(dom * strip, dtype=jnp.int32)
    line = (line // strip) * own_rows + line % strip - 1
    inside = (line >= 0) & (line < height)
    rows = jnp.arange(height, dtype=jnp.int32)
    cols = jnp.arange(width, dtype=jnp.int32)
    row_sel = (
        (rows[None, None, :] == line[None, :, None] + centers[:, 0, None, None]) & inside[None, :, None]
    ).astype(jnp.bfloat16)
    col_sel = (cols[None, None, :] == cols[None, :, None] + centers[:, 1, None, None]).astype(jnp.bfloat16)
    moved = jnp.einsum("kua,kav->kuv", row_sel, particles, preferred_element_type=jnp.float32).astype(jnp.bfloat16)
    strips = jnp.einsum("kub,kvb->kuv", moved, col_sel, preferred_element_type=jnp.float32).astype(jnp.bfloat16)
    strips = strips.reshape(count, dom, strip, width).transpose(1, 2, 0, 3)
    notes = jnp.concatenate([groups, rot_prior[:, None]], axis=1).astype(jnp.bfloat16)
    notes = jnp.pad(notes, ((0, 0), (0, width - notes.shape[1])))
    strips = jnp.concatenate([strips, jnp.broadcast_to(notes, (dom, 1, count, width))], axis=1)

    refs = references.reshape(dim_j // 16, 16, pixels)
    share = -(-18 * dim_j // (16 * dom)) * 16
    half = ring // 2
    block = refs.shape
    shifted, part, meta = pl.pallas_call(
        functools.partial(score_kernel, dom, ring),
        out_shape=(
            jax.ShapeDtypeStruct((9 * slots, pixels), jnp.bfloat16),
            jax.ShapeDtypeStruct((dom * share, slots), jnp.float32),
            jax.ShapeDtypeStruct((8, slots), jnp.int32),
        ),
        in_specs=[VMEM] * 2,
        out_specs=(VMEM, VMEM, VMEM),
        scratch_shapes=[
            pltpu.VMEM((ring,) + block, jnp.bfloat16),
            pltpu.VMEM(strips.shape, jnp.bfloat16),
            pltpu.VMEM((2 * dim_j, 9 * slots), jnp.float32),
        ]
        + [sem((half, block[0]))] * 4
        + [sem((dom,)), sem((dom,)), sem((2,))],
        compiler_params=pltpu.CompilerParams(collective_id=0, has_side_effects=True),
    )(refs, strips)

    like, stat = pl.pallas_call(
        functools.partial(evidence_kernel, dom, rotations, 18 * dim_j),
        out_shape=(
            jax.ShapeDtypeStruct((dom, share, slots), jnp.bfloat16),
            jax.ShapeDtypeStruct((dom, 2, slots), jnp.float32),
        ),
        in_specs=[VMEM] * 2,
        out_specs=(VMEM, VMEM),
        scratch_shapes=[pltpu.VMEM((dom // 2, share, slots), jnp.float32)] * 2 + [sem((12, dom // 2))],
        compiler_params=pltpu.CompilerParams(collective_id=1, has_side_effects=True),
    )(part.reshape(dom, share, slots), meta)

    total, evidence = pl.pallas_call(
        functools.partial(sums_kernel, ring),
        out_shape=(
            jax.ShapeDtypeStruct(block, jnp.float32),
            jax.ShapeDtypeStruct((1, count), jnp.float32),
        ),
        in_specs=[VMEM] * 4,
        out_specs=(VMEM, VMEM),
        scratch_shapes=[
            pltpu.VMEM((dom * share, slots), jnp.bfloat16),
            pltpu.VMEM((2 * dim_j, 9 * slots), jnp.bfloat16),
            pltpu.VMEM((ring,) + block, jnp.bfloat16),
        ]
        + [pltpu.VMEM((half,) + block, jnp.bfloat16)] * 2
        + [sem((half, block[0]))] * 4,
        compiler_params=pltpu.CompilerParams(collective_id=2, has_side_effects=True),
    )(like, stat, meta, shifted)
    class_sums = total.reshape(references.shape[0], rotations, pixels).transpose(2, 0, 1)
    return class_sums, evidence.reshape(count)


def solution(mesh):
    placed = (
        P(("dom", "cls"), None, None),
        P(("dom", "cls"), None),
        P(("dom", "cls")),
        P(("dom", "cls"), None),
        P("cls", None, "dom"),
    )
    return jax.shard_map(
        per_device,
        mesh=mesh,
        in_specs=placed,
        out_specs=(P("dom", "cls", None), P(("dom", "cls"))),
        check_vma=False,
    )
```

```python
import functools

import jax
import jax.numpy as jnp
from jax import lax
from jax.experimental import pallas as pl
from jax.experimental.pallas import tpu as pltpu
from jax.sharding import PartitionSpec as P

LAMBDA = 1.0
NEG_BIG = -1e30
LANES = 128
VMEM = pl.BlockSpec(memory_space=pltpu.VMEM)
MESH = pl.DeviceIdType.MESH


def remote(src, dst, send_sem, recv_sem, peer):
    return pltpu.make_async_remote_copy(
        src_ref=src, dst_ref=dst, send_sem=send_sem, recv_sem=recv_sem, device_id=peer, device_id_type=MESH
    )


def signal_all(peers, ring):
    barrier = pltpu.get_barrier_semaphore()
    total = 0
    if peers is not None:
        first, last, name = peers

        def one(k, carry):
            pl.semaphore_signal(barrier, inc=1, device_id={"dom": name(k)}, device_id_type=MESH)
            return carry

        lax.fori_loop(first, last, one, 0)
        total += last - first
    if ring:
        z = lax.axis_index("cls")
        for step in (1, ring - 1):
            pl.semaphore_signal(barrier, inc=1, device_id={"cls": lax.rem(z + step, ring)}, device_id_type=MESH)
        total += 2
    return barrier, total


def greet(peers, ring):
    barrier, total = signal_all(peers, ring)
    pl.semaphore_wait(barrier, total)


def chunks(blocks):
    return [(c, 1) for c in range(blocks)]


def each(first, last, fn):
    def body(k, carry):
        fn(k)
        return carry

    lax.fori_loop(first, last, body, 0)


def score_kernel(dom, ring, refs, imgs, shifted, out, meta, all_refs, all_imgs, turned, score, rs, rr, ls, lr, ds, dr, local):
    d = lax.axis_index("dom")
    z = lax.axis_index("cls")
    right, left = lax.rem(z + 1, ring), lax.rem(z + ring - 1, ring)
    blocks, sixteen, pixels = refs.shape
    dim_j = blocks * sixteen
    strip, count, width = imgs.shape[1:]
    own_rows = strip - 3
    slots = dom * count
    steps_r = ring // 2
    steps_l = ring - 1 - steps_r
    greet((1, dom, lambda k: lax.rem(d + k, dom)), ring)
    own = pltpu.make_async_copy(refs, all_refs.at[z], local.at[0])
    own.start()
    mine = pltpu.make_async_copy(imgs.at[d], all_imgs.at[d], local.at[1])
    mine.start()

    def hop(step, c, to_right, src=None):
        piece = lax.rem(z + ring - step, ring) if to_right else lax.rem(z + step, ring)
        block = all_refs.at[piece, c]
        send, recv = (rs, rr) if to_right else (ls, lr)
        return remote(
            block if src is None else src, block, send.at[step, c], recv.at[step, c],
            {"cls": right if to_right else left},
        )

    for c in range(blocks):
        for to_right in (True, False):
            hop(0, c, to_right, refs.at[c]).start()

    def sent_strip(k):
        peer = lax.rem(d + k, dom)
        return remote(imgs.at[peer], all_imgs.at[d], ds.at[k], dr.at[k], {"dom": peer})

    each(1, dom, lambda k: sent_strip(k).start())
    out[...] = jnp.zeros_like(out)

    def forward(step, to_left):
        for c in range(blocks):
            hop(step - 1, c, True).wait_recv()
            hop(step, c, True).start()
            hop(step - 1, c, False).wait_recv()
            if to_left:
                hop(step, c, False).start()

    forward(1, True)
    each(1, dom, lambda k: sent_strip(k).wait())
    mine.wait()
    own.wait()
    forward(2, True)
    lane = lax.broadcasted_iota(jnp.int32, (slots, width), 1)
    line = lax.broadcasted_iota(jnp.int32, (width, slots), 0)
    for h in range(own_rows + 2):
        mid = all_imgs[:, h].astype(jnp.float32).reshape(slots, width)
        before = jnp.where(lane == 0, 0.0, pltpu.roll(mid, 1, axis=1))
        after = jnp.where(lane == width - 1, 0.0, pltpu.roll(mid, width - 1, axis=1))
        mid_t = jnp.transpose(mid)
        before_t = jnp.where(line == 0, 0.0, pltpu.roll(mid_t, 1, axis=0))
        after_t = jnp.where(line == width - 1, 0.0, pltpu.roll(mid_t, width - 1, axis=0))
        for sy, (plane, plane_t) in enumerate(((before, before_t), (mid, mid_t), (after, after_t))):
            plane = plane.astype(jnp.bfloat16)
            plane_t = plane_t.astype(jnp.bfloat16)
            for sx in range(3):
                r = h - sx
                if 0 <= r < own_rows:
                    first = (3 * sx + sy) * slots
                    shifted[first:first + slots, r * width:(r + 1) * width] = plane
                    turned[r * width:(r + 1) * width, first:first + slots] = plane_t
    notes = all_imgs[:, strip - 1].astype(jnp.float32).reshape(slots, width)
    meta[...] = jnp.transpose(notes)[:8].astype(jnp.int32)
    names = [jnp.broadcast_to(meta[t:t + 1, :], (dim_j, slots)) for t in range(2)]

    def pair(ga, gb):
        both = jnp.concatenate(
            [all_refs[ga].reshape(dim_j, pixels), all_refs[gb].reshape(dim_j, pixels)], axis=0
        )
        score[...] = jnp.dot(both, turned[...], preferred_element_type=jnp.float32)
        wide = both.astype(jnp.float32)
        bias = -0.5 * jnp.sum(wide * wide, axis=1, keepdims=True)

        def pick(w):
            cols = pl.ds(pl.multiple_of(w * slots, LANES), slots)
            first = score[0:dim_j, cols] + bias[:dim_j]
            second = score[dim_j:, cols] + bias[dim_j:]
            for t in range(2):
                rows = pl.ds(pl.multiple_of((t * 9 + w) * dim_j, 16), dim_j)
                out[rows, :] = jnp.where(
                    names[t] == ga, first, jnp.where(names[t] == gb, second, out[rows, :])
                )

        each(0, 9, pick)

    def near(step):
        pair(lax.rem(z + ring - step, ring), lax.rem(z + step, ring))

    forward(3, True)
    each(1, 3, near)

    def middle(step):
        forward(step, True)
        near(step - 1)

    each(4, steps_l, middle)
    forward(steps_l, False)
    each(steps_l - 1, steps_l + 1, near)
    for c in range(blocks):
        hop(steps_r - 1, c, True).wait_recv()
    pair(lax.rem(z + steps_r, ring), z)

    def drain(step):
        for c in range(blocks):
            hop(step, c, True).wait_send()

    def drain_left(step):
        for c in range(blocks):
            hop(step, c, False).wait_send()

    each(0, steps_r, drain)
    each(0, steps_l, drain_left)


def evidence_kernel(dom, rotations, used, part, meta, like, stat, held, landed, sems):
    d = lax.axis_index("dom")
    core = lax.rem(d, 2)
    chip = d // 2
    chips = dom // 2
    other = chip * 2 + 1 - core

    def at(k):
        return lax.rem(chip + k, chips)

    def back(k):
        return lax.rem(chip + chips - k, chips)

    barrier, total = signal_all((1, chips, lambda k: at(k) * 2 + core), 0)
    pl.semaphore_signal(barrier, inc=1, device_id={"dom": other}, device_id_type=MESH)
    pl.semaphore_wait(barrier, total + 1)

    def swap(k):
        return remote(part.at[at(k) * 2 + 1 - core], held.at[at(k)], sems.at[0, k], sems.at[1, k], {"dom": other})

    def scatter(k):
        return remote(held.at[at(k)], landed.at[chip], sems.at[2, k], sems.at[3, k], {"dom": at(k) * 2 + core})

    def across(ref, first, k):
        return remote(ref.at[d], ref.at[d], sems.at[first, k], sems.at[first + 1, k], {"dom": at(k) * 2 + core})

    def onward(ref, first, k):
        block = ref.at[back(k) * 2 + core]
        return remote(block, block, sems.at[first, k], sems.at[first + 1, k], {"dom": other})

    each(1, chips, lambda k: swap(k).start())
    swap(0).start()

    def merge(k):
        swap(k).wait_recv()
        held[at(k)] += part[at(k) * 2 + core]

    merge(1)

    def step(k):
        merge(k)
        scatter(k - 1).start()

    each(2, chips, step)
    merge(0)
    scatter(chips - 1).start()

    def take(k, carry):
        scatter(k).wait_recv()
        return carry + landed[back(k)]

    total = lax.fori_loop(1, chips, take, held[chip])
    row = lax.broadcasted_iota(jnp.int32, total.shape, 0)
    prior = jnp.broadcast_to(meta[2:3, :], total.shape)
    delta = jnp.abs(row % rotations - prior)
    dist = jnp.minimum(delta, rotations - delta).astype(jnp.float32)
    valid = row + d * total.shape[0] < used
    loglik = jnp.where(valid, total - LAMBDA * dist * dist, NEG_BIG)
    top = jnp.max(loglik, axis=0, keepdims=True)
    value = jnp.where(valid, jnp.exp(loglik - top), 0.0)
    like[d] = value.astype(jnp.bfloat16)
    mass = jnp.sum(value, axis=0, keepdims=True)
    pick = lax.broadcasted_iota(jnp.int32, stat.shape[1:], 0)
    stat[d] = jnp.where(pick == 0, top, mass)
    each(0, chips, lambda k: swap(k).wait_send())

    def give(k):
        scatter(k).wait_send()
        across(like, 4, k).start()
        across(stat, 6, k).start()

    each(1, chips, give)
    onward(like, 8, 0).start()
    onward(stat, 10, 0).start()

    def relay(k):
        across(like, 4, k).wait_recv()
        onward(like, 8, k).start()
        across(stat, 6, k).wait_recv()
        onward(stat, 10, k).start()

    each(1, chips, relay)

    def finish(k):
        onward(like, 8, k).wait()
        onward(stat, 10, k).wait()

    each(0, chips, finish)

    def sent(k):
        across(like, 4, k).wait_send()
        across(stat, 6, k).wait_send()

    each(1, chips, sent)


def sums_kernel(ring, like, stat, meta, shifted, out, evidence, post, dense, part, from_left, from_right, rs, rr, ls, lr):
    z = lax.axis_index("cls")
    right, left = lax.rem(z + 1, ring), lax.rem(z + ring - 1, ring)
    barrier, greetings = signal_all(None, ring)
    dom, rows, slots = like.shape
    blocks, sixteen, pixels = out.shape
    dim_j = blocks * sixteen
    steps_r = ring // 2
    steps_l = ring - 1 - steps_r
    top = stat[:, 0, :]
    mass = stat[:, 1, :]
    peak = jnp.max(top, axis=0, keepdims=True)
    total = jnp.sum(mass * jnp.exp(top - peak), axis=0, keepdims=True)
    ev = peak + jnp.log(total)
    count = evidence.shape[1]
    turn = lax.rem(slots - lax.axis_index("dom") * count, slots)
    evidence[...] = pltpu.roll(jnp.broadcast_to(ev, (8, slots)), turn, axis=1)[0:1, :count]

    def scale(k):
        factor = jnp.exp(stat[k, 0:1, :] - ev)
        post[pl.ds(pl.multiple_of(k * rows, 16), rows), :] = (like[k].astype(jnp.float32) * factor).astype(jnp.bfloat16)

    each(0, dom, scale)
    names = [jnp.broadcast_to(meta[t:t + 1, :], (dim_j, slots)) for t in range(2)]

    def pair(ga, gb):
        for w in range(9):
            p0 = post[w * dim_j:(w + 1) * dim_j, :].astype(jnp.float32)
            p1 = post[(9 + w) * dim_j:(10 + w) * dim_j, :].astype(jnp.float32)
            for first, g in ((0, ga), (dim_j, gb)):
                weight = jnp.where(names[0] == g, p0, jnp.where(names[1] == g, p1, 0.0))
                dense[first:first + dim_j, w * slots:(w + 1) * slots] = weight.astype(jnp.bfloat16)
        sums = jnp.dot(dense[...], shifted[...], preferred_element_type=jnp.float32).astype(jnp.bfloat16)
        part[ga] = sums[:dim_j].reshape(blocks, sixteen, pixels)
        part[gb] = sums[dim_j:].reshape(blocks, sixteen, pixels)

    def hop(step, c, to_right, src=None):
        hold, send, recv = (from_left, rs, rr) if to_right else (from_right, ls, lr)
        return remote(
            hold.at[step - 1, c] if src is None else src, hold.at[step, c], send.at[step, c], recv.at[step, c],
            {"cls": right if to_right else left},
        )

    def add_on(step, c, to_right, owner):
        hold = from_left if to_right else from_right
        hop(step - 1, c, to_right, part.at[owner, c]).wait_recv()
        hold[step - 1, c] = (
            hold[step - 1, c].astype(jnp.float32) + part[owner, c].astype(jnp.float32)
        ).astype(jnp.bfloat16)
        hop(step, c, to_right).start()

    far = lax.rem(z + steps_r, ring)
    pair(far, z)
    pl.semaphore_wait(barrier, greetings)
    for c in range(blocks):
        hop(0, c, True, part.at[far, c]).start()

    def owners(i):
        return lax.rem(z + steps_l - i, ring), lax.rem(z + ring - steps_l + i, ring)

    first_r, first_l = owners(0)
    pair(first_r, first_l)
    for c in range(blocks):
        hop(0, c, False, part.at[first_l, c]).start()
    for c in range(blocks):
        add_on(1, c, True, first_r)

    def step(i):
        owner_r, owner_l = owners(i)
        pair(owner_r, owner_l)
        for c in range(blocks):
            add_on(i, c, False, owner_l)
            add_on(i + 1, c, True, owner_r)

    each(1, steps_l, step)
    for c in range(blocks):
        hop(steps_r - 1, c, True).wait_recv()
        hop(steps_l - 1, c, False).wait_recv()
        out[c] = (
            part[z, c].astype(jnp.float32)
            + from_left[steps_r - 1, c].astype(jnp.float32)
            + from_right[steps_l - 1, c].astype(jnp.float32)
        )
    for to_right, steps in ((True, steps_r), (False, steps_l)):
        for c in range(blocks):
            hop(0, c, to_right, part.at[z, c]).wait_send()

        def drain(i):
            for c in range(blocks):
                hop(i, c, to_right).wait_send()

        each(1, steps, drain)


def per_device(particles, centers, rot_prior, groups, references):
    count, height, width = particles.shape
    dom = lax.axis_size("dom")
    ring = lax.axis_size("cls")
    rotations = references.shape[1]
    dim_j = references.shape[0] * rotations
    own_rows = height // dom
    pixels = own_rows * width
    strip = own_rows + 2
    slots = dom * count
    sem = pltpu.SemaphoreType.DMA

    line = jnp.arange(dom * strip, dtype=jnp.int32)
    line = (line // strip) * own_rows + line % strip - 1
    inside = (line >= 0) & (line < height)
    rows = jnp.arange(height, dtype=jnp.int32)
    cols = jnp.arange(width, dtype=jnp.int32)
    row_sel = (
        (rows[None, None, :] == line[None, :, None] + centers[:, 0, None, None]) & inside[None, :, None]
    ).astype(jnp.bfloat16)
    col_sel = (cols[None, None, :] == cols[None, :, None] + centers[:, 1, None, None]).astype(jnp.bfloat16)
    moved = jnp.einsum("kua,kav->kuv", row_sel, particles, preferred_element_type=jnp.float32).astype(jnp.bfloat16)
    strips = jnp.einsum("kub,kvb->kuv", moved, col_sel, preferred_element_type=jnp.float32).astype(jnp.bfloat16)
    strips = strips.reshape(count, dom, strip, width).transpose(1, 2, 0, 3)
    notes = jnp.concatenate([groups, rot_prior[:, None]], axis=1).astype(jnp.bfloat16)
    notes = jnp.pad(notes, ((0, 0), (0, width - notes.shape[1])))
    strips = jnp.concatenate([strips, jnp.broadcast_to(notes, (dom, 1, count, width))], axis=1)

    refs = references.reshape(dim_j // 16, 16, pixels)
    share = -(-18 * dim_j // (16 * dom)) * 16
    half = ring // 2
    block = refs.shape
    shifted, part, meta = pl.pallas_call(
        functools.partial(score_kernel, dom, ring),
        out_shape=(
            jax.ShapeDtypeStruct((9 * slots, pixels), jnp.bfloat16),
            jax.ShapeDtypeStruct((dom * share, slots), jnp.float32),
            jax.ShapeDtypeStruct((8, slots), jnp.int32),
        ),
        in_specs=[VMEM] * 2,
        out_specs=(VMEM, VMEM, VMEM),
        scratch_shapes=[
            pltpu.VMEM((ring,) + block, jnp.bfloat16),
            pltpu.VMEM(strips.shape, jnp.bfloat16),
            pltpu.VMEM((pixels, 9 * slots), jnp.bfloat16),
            pltpu.VMEM((2 * dim_j, 9 * slots), jnp.float32),
        ]
        + [sem((half, block[0]))] * 4
        + [sem((dom,)), sem((dom,)), sem((2,))],
        compiler_params=pltpu.CompilerParams(collective_id=0, has_side_effects=True),
    )(refs, strips)

    like, stat = pl.pallas_call(
        functools.partial(evidence_kernel, dom, rotations, 18 * dim_j),
        out_shape=(
            jax.ShapeDtypeStruct((dom, share, slots), jnp.bfloat16),
            jax.ShapeDtypeStruct((dom, 2, slots), jnp.float32),
        ),
        in_specs=[VMEM] * 2,
        out_specs=(VMEM, VMEM),
        scratch_shapes=[pltpu.VMEM((dom // 2, share, slots), jnp.float32)] * 2 + [sem((12, dom // 2))],
        compiler_params=pltpu.CompilerParams(collective_id=1, has_side_effects=True),
    )(part.reshape(dom, share, slots), meta)

    total, evidence = pl.pallas_call(
        functools.partial(sums_kernel, ring),
        out_shape=(
            jax.ShapeDtypeStruct(block, jnp.float32),
            jax.ShapeDtypeStruct((1, count), jnp.float32),
        ),
        in_specs=[VMEM] * 4,
        out_specs=(VMEM, VMEM),
        scratch_shapes=[
            pltpu.VMEM((dom * share, slots), jnp.bfloat16),
            pltpu.VMEM((2 * dim_j, 9 * slots), jnp.bfloat16),
            pltpu.VMEM((ring,) + block, jnp.bfloat16),
        ]
        + [pltpu.VMEM((half,) + block, jnp.bfloat16)] * 2
        + [sem((half, block[0]))] * 4,
        compiler_params=pltpu.CompilerParams(collective_id=2, has_side_effects=True),
    )(like, stat, meta, shifted)
    class_sums = total.reshape(references.shape[0], rotations, pixels).transpose(2, 0, 1)
    return class_sums, evidence.reshape(count)


def solution(mesh):
    placed = (
        P(("dom", "cls"), None, None),
        P(("dom", "cls"), None),
        P(("dom", "cls")),
        P(("dom", "cls"), None),
        P("cls", None, "dom"),
    )
    return jax.shard_map(
        per_device,
        mesh=mesh,
        in_specs=placed,
        out_specs=(P("dom", "cls", None), P(("dom", "cls"))),
        check_vma=False,
    )
```

```python
import functools

import jax
import jax.numpy as jnp
from jax import lax
from jax.experimental import pallas as pl
from jax.experimental.pallas import tpu as pltpu
from jax.sharding import PartitionSpec as P

LAMBDA = 1.0
NEG_BIG = -1e30
LANES = 128
STRIDE = 11
VMEM = pl.BlockSpec(memory_space=pltpu.VMEM)
MESH = pl.DeviceIdType.MESH


def remote(src, dst, send_sem, recv_sem, peer):
    return pltpu.make_async_remote_copy(
        src_ref=src, dst_ref=dst, send_sem=send_sem, recv_sem=recv_sem, device_id=peer, device_id_type=MESH
    )


def signal_all(peers, ring):
    barrier = pltpu.get_barrier_semaphore()
    total = 0
    if peers is not None:
        first, last, name = peers

        def one(k, carry):
            pl.semaphore_signal(barrier, inc=1, device_id={"dom": name(k)}, device_id_type=MESH)
            return carry

        lax.fori_loop(first, last, one, 0)
        total += last - first
    if ring:
        z = lax.axis_index("cls")
        for step in (1, ring - 1):
            pl.semaphore_signal(barrier, inc=1, device_id={"cls": lax.rem(z + step, ring)}, device_id_type=MESH)
        total += 2
    return barrier, total


def greet(peers, ring):
    barrier, total = signal_all(peers, ring)
    pl.semaphore_wait(barrier, total)


def chunks(blocks):
    return [(c, 1) for c in range(blocks)]


def each(first, last, fn):
    def body(k, carry):
        fn(k)
        return carry

    lax.fori_loop(first, last, body, 0)


def score_kernel(dom, ring, refs, imgs, shifted, out, meta, all_refs, all_imgs, turned, score, rs, rr, ls, lr, ds, dr, local):
    d = lax.axis_index("dom")
    z = lax.axis_index("cls")
    right, left = lax.rem(z + 1, ring), lax.rem(z + ring - 1, ring)
    blocks, sixteen, pixels = refs.shape
    dim_j = blocks * sixteen
    strip, count, width = imgs.shape[1:]
    own_rows = strip - 3
    slots = dom * count
    steps_r = ring // 2
    steps_l = ring - 1 - steps_r
    greet((1, dom, lambda k: lax.rem(d + k, dom)), ring)
    own = pltpu.make_async_copy(refs, all_refs.at[z], local.at[0])
    own.start()
    mine = pltpu.make_async_copy(imgs.at[d], all_imgs.at[d], local.at[1])
    mine.start()

    def hop(step, c, to_right, src=None):
        piece = lax.rem(z + ring - step, ring) if to_right else lax.rem(z + step, ring)
        block = all_refs.at[piece, c]
        send, recv = (rs, rr) if to_right else (ls, lr)
        return remote(
            block if src is None else src, block, send.at[step, c], recv.at[step, c],
            {"cls": right if to_right else left},
        )

    for c in range(blocks):
        for to_right in (True, False):
            hop(0, c, to_right, refs.at[c]).start()

    def sent_strip(k):
        peer = lax.rem(d + STRIDE * k, dom)
        return remote(imgs.at[peer], all_imgs.at[d], ds.at[k], dr.at[k], {"dom": peer})

    each(1, dom, lambda k: sent_strip(k).start())
    out[...] = jnp.zeros_like(out)

    def forward(step, to_left):
        for c in range(blocks):
            hop(step - 1, c, True).wait_recv()
            hop(step, c, True).start()
            hop(step - 1, c, False).wait_recv()
            if to_left:
                hop(step, c, False).start()

    forward(1, True)
    each(1, dom, lambda k: sent_strip(k).wait())
    mine.wait()
    own.wait()
    forward(2, True)
    lane = lax.broadcasted_iota(jnp.int32, (slots, width), 1)
    line = lax.broadcasted_iota(jnp.int32, (width, slots), 0)
    for h in range(own_rows + 2):
        mid = all_imgs[:, h].astype(jnp.float32).reshape(slots, width)
        before = jnp.where(lane == 0, 0.0, pltpu.roll(mid, 1, axis=1))
        after = jnp.where(lane == width - 1, 0.0, pltpu.roll(mid, width - 1, axis=1))
        mid_t = jnp.transpose(mid)
        before_t = jnp.where(line == 0, 0.0, pltpu.roll(mid_t, 1, axis=0))
        after_t = jnp.where(line == width - 1, 0.0, pltpu.roll(mid_t, width - 1, axis=0))
        for sy, (plane, plane_t) in enumerate(((before, before_t), (mid, mid_t), (after, after_t))):
            plane = plane.astype(jnp.bfloat16)
            plane_t = plane_t.astype(jnp.bfloat16)
            for sx in range(3):
                r = h - sx
                if 0 <= r < own_rows:
                    first = (3 * sx + sy) * slots
                    shifted[first:first + slots, r * width:(r + 1) * width] = plane
                    turned[r * width:(r + 1) * width, first:first + slots] = plane_t
    notes = all_imgs[:, strip - 1].astype(jnp.float32).reshape(slots, width)
    meta[...] = jnp.transpose(notes)[:8].astype(jnp.int32)
    names = [jnp.broadcast_to(meta[t:t + 1, :], (dim_j, slots)) for t in range(2)]

    def pair(ga, gb):
        both = jnp.concatenate(
            [all_refs[ga].reshape(dim_j, pixels), all_refs[gb].reshape(dim_j, pixels)], axis=0
        )
        score[...] = jnp.dot(both, turned[...], preferred_element_type=jnp.float32)
        wide = both.astype(jnp.float32)
        bias = -0.5 * jnp.sum(wide * wide, axis=1, keepdims=True)

        def pick(w):
            cols = pl.ds(pl.multiple_of(w * slots, LANES), slots)
            first = score[0:dim_j, cols] + bias[:dim_j]
            second = score[dim_j:, cols] + bias[dim_j:]
            for t in range(2):
                rows = pl.ds(pl.multiple_of((t * 9 + w) * dim_j, 16), dim_j)
                out[rows, :] = jnp.where(
                    names[t] == ga, first, jnp.where(names[t] == gb, second, out[rows, :])
                )

        each(0, 9, pick)

    def near(step):
        pair(lax.rem(z + ring - step, ring), lax.rem(z + step, ring))

    forward(3, True)
    each(1, 3, near)

    def middle(step):
        forward(step, True)
        near(step - 1)

    each(4, steps_l, middle)
    forward(steps_l, False)
    each(steps_l - 1, steps_l + 1, near)
    for c in range(blocks):
        hop(steps_r - 1, c, True).wait_recv()
    pair(lax.rem(z + steps_r, ring), z)

    def drain(step):
        for c in range(blocks):
            hop(step, c, True).wait_send()

    def drain_left(step):
        for c in range(blocks):
            hop(step, c, False).wait_send()

    each(0, steps_r, drain)
    each(0, steps_l, drain_left)


def evidence_kernel(dom, rotations, used, part, meta, like, stat, held, landed, sems):
    d = lax.axis_index("dom")
    core = lax.rem(d, 2)
    chip = d // 2
    chips = dom // 2
    other = chip * 2 + 1 - core

    def at(k):
        return lax.rem(chip + STRIDE * k, chips)

    def back(k):
        return lax.rem(chip + STRIDE * (chips - k), chips)

    barrier, total = signal_all((1, chips, lambda k: at(k) * 2 + core), 0)
    pl.semaphore_signal(barrier, inc=1, device_id={"dom": other}, device_id_type=MESH)
    pl.semaphore_wait(barrier, total + 1)

    def swap(k):
        return remote(part.at[at(k) * 2 + 1 - core], held.at[at(k)], sems.at[0, k], sems.at[1, k], {"dom": other})

    def scatter(k):
        return remote(held.at[at(k)], landed.at[chip], sems.at[2, k], sems.at[3, k], {"dom": at(k) * 2 + core})

    def across(ref, first, k):
        return remote(ref.at[d], ref.at[d], sems.at[first, k], sems.at[first + 1, k], {"dom": at(k) * 2 + core})

    def onward(ref, first, k):
        block = ref.at[back(k) * 2 + core]
        return remote(block, block, sems.at[first, k], sems.at[first + 1, k], {"dom": other})

    each(1, chips, lambda k: swap(k).start())
    swap(0).start()

    def merge(k):
        swap(k).wait_recv()
        held[at(k)] += part[at(k) * 2 + core]

    merge(1)

    def step(k):
        merge(k)
        scatter(k - 1).start()

    each(2, chips, step)
    merge(0)
    scatter(chips - 1).start()

    def take(k, carry):
        scatter(k).wait_recv()
        return carry + landed[back(k)]

    total = lax.fori_loop(1, chips, take, held[chip])
    row = lax.broadcasted_iota(jnp.int32, total.shape, 0)
    prior = jnp.broadcast_to(meta[2:3, :], total.shape)
    delta = jnp.abs(row % rotations - prior)
    dist = jnp.minimum(delta, rotations - delta).astype(jnp.float32)
    valid = row + d * total.shape[0] < used
    loglik = jnp.where(valid, total - LAMBDA * dist * dist, NEG_BIG)
    top = jnp.max(loglik, axis=0, keepdims=True)
    value = jnp.where(valid, jnp.exp(loglik - top), 0.0)
    like[d] = value.astype(jnp.bfloat16)
    mass = jnp.sum(value, axis=0, keepdims=True)
    pick = lax.broadcasted_iota(jnp.int32, stat.shape[1:], 0)
    stat[d] = jnp.where(pick == 0, top, mass)
    each(0, chips, lambda k: swap(k).wait_send())

    def give(k):
        scatter(k).wait_send()
        across(like, 4, k).start()
        across(stat, 6, k).start()

    each(1, chips, give)
    onward(like, 8, 0).start()
    onward(stat, 10, 0).start()

    def relay(k):
        across(like, 4, k).wait_recv()
        onward(like, 8, k).start()
        across(stat, 6, k).wait_recv()
        onward(stat, 10, k).start()

    each(1, chips, relay)

    def finish(k):
        onward(like, 8, k).wait()
        onward(stat, 10, k).wait()

    each(0, chips, finish)

    def sent(k):
        across(like, 4, k).wait_send()
        across(stat, 6, k).wait_send()

    each(1, chips, sent)


def sums_kernel(ring, like, stat, meta, shifted, out, evidence, post, dense, part, from_left, from_right, rs, rr, ls, lr):
    z = lax.axis_index("cls")
    right, left = lax.rem(z + 1, ring), lax.rem(z + ring - 1, ring)
    barrier, greetings = signal_all(None, ring)
    dom, rows, slots = like.shape
    blocks, sixteen, pixels = out.shape
    dim_j = blocks * sixteen
    steps_r = ring // 2
    steps_l = ring - 1 - steps_r
    top = stat[:, 0, :]
    mass = stat[:, 1, :]
    peak = jnp.max(top, axis=0, keepdims=True)
    total = jnp.sum(mass * jnp.exp(top - peak), axis=0, keepdims=True)
    ev = peak + jnp.log(total)
    count = evidence.shape[1]
    turn = lax.rem(slots - lax.axis_index("dom") * count, slots)
    evidence[...] = pltpu.roll(jnp.broadcast_to(ev, (8, slots)), turn, axis=1)[0:1, :count]

    def scale(k):
        factor = jnp.exp(stat[k, 0:1, :] - ev)
        post[pl.ds(pl.multiple_of(k * rows, 16), rows), :] = (like[k].astype(jnp.float32) * factor).astype(jnp.bfloat16)

    each(0, dom, scale)
    names = [jnp.broadcast_to(meta[t:t + 1, :], (dim_j, slots)) for t in range(2)]

    def pair(ga, gb):
        for w in range(9):
            p0 = post[w * dim_j:(w + 1) * dim_j, :].astype(jnp.float32)
            p1 = post[(9 + w) * dim_j:(10 + w) * dim_j, :].astype(jnp.float32)
            for first, g in ((0, ga), (dim_j, gb)):
                weight = jnp.where(names[0] == g, p0, jnp.where(names[1] == g, p1, 0.0))
                dense[first:first + dim_j, w * slots:(w + 1) * slots] = weight.astype(jnp.bfloat16)
        sums = jnp.dot(dense[...], shifted[...], preferred_element_type=jnp.float32).astype(jnp.bfloat16)
        part[ga] = sums[:dim_j].reshape(blocks, sixteen, pixels)
        part[gb] = sums[dim_j:].reshape(blocks, sixteen, pixels)

    def hop(step, c, to_right, src=None):
        hold, send, recv = (from_left, rs, rr) if to_right else (from_right, ls, lr)
        return remote(
            hold.at[step - 1, c] if src is None else src, hold.at[step, c], send.at[step, c], recv.at[step, c],
            {"cls": right if to_right else left},
        )

    def add_on(step, c, to_right, owner):
        hold = from_left if to_right else from_right
        hop(step - 1, c, to_right, part.at[owner, c]).wait_recv()
        hold[step - 1, c] = (
            hold[step - 1, c].astype(jnp.float32) + part[owner, c].astype(jnp.float32)
        ).astype(jnp.bfloat16)
        hop(step, c, to_right).start()

    far = lax.rem(z + steps_r, ring)
    pair(far, z)
    pl.semaphore_wait(barrier, greetings)
    for c in range(blocks):
        hop(0, c, True, part.at[far, c]).start()

    def owners(i):
        return lax.rem(z + steps_l - i, ring), lax.rem(z + ring - steps_l + i, ring)

    first_r, first_l = owners(0)
    pair(first_r, first_l)
    for c in range(blocks):
        hop(0, c, False, part.at[first_l, c]).start()
    for c in range(blocks):
        add_on(1, c, True, first_r)

    def step(i):
        owner_r, owner_l = owners(i)
        pair(owner_r, owner_l)
        for c in range(blocks):
            add_on(i, c, False, owner_l)
            add_on(i + 1, c, True, owner_r)

    each(1, steps_l, step)
    for c in range(blocks):
        hop(steps_r - 1, c, True).wait_recv()
        hop(steps_l - 1, c, False).wait_recv()
        out[c] = (
            part[z, c].astype(jnp.float32)
            + from_left[steps_r - 1, c].astype(jnp.float32)
            + from_right[steps_l - 1, c].astype(jnp.float32)
        )
    for to_right, steps in ((True, steps_r), (False, steps_l)):
        for c in range(blocks):
            hop(0, c, to_right, part.at[z, c]).wait_send()

        def drain(i):
            for c in range(blocks):
                hop(i, c, to_right).wait_send()

        each(1, steps, drain)


def per_device(particles, centers, rot_prior, groups, references):
    count, height, width = particles.shape
    dom = lax.axis_size("dom")
    ring = lax.axis_size("cls")
    rotations = references.shape[1]
    dim_j = references.shape[0] * rotations
    own_rows = height // dom
    pixels = own_rows * width
    strip = own_rows + 2
    slots = dom * count
    sem = pltpu.SemaphoreType.DMA

    line = jnp.arange(dom * strip, dtype=jnp.int32)
    line = (line // strip) * own_rows + line % strip - 1
    inside = (line >= 0) & (line < height)
    rows = jnp.arange(height, dtype=jnp.int32)
    cols = jnp.arange(width, dtype=jnp.int32)
    row_sel = (
        (rows[None, None, :] == line[None, :, None] + centers[:, 0, None, None]) & inside[None, :, None]
    ).astype(jnp.bfloat16)
    col_sel = (cols[None, None, :] == cols[None, :, None] + centers[:, 1, None, None]).astype(jnp.bfloat16)
    moved = jnp.einsum("kua,kav->kuv", row_sel, particles, preferred_element_type=jnp.float32).astype(jnp.bfloat16)
    strips = jnp.einsum("kub,kvb->kuv", moved, col_sel, preferred_element_type=jnp.float32).astype(jnp.bfloat16)
    strips = strips.reshape(count, dom, strip, width).transpose(1, 2, 0, 3)
    notes = jnp.concatenate([groups, rot_prior[:, None]], axis=1).astype(jnp.bfloat16)
    notes = jnp.pad(notes, ((0, 0), (0, width - notes.shape[1])))
    strips = jnp.concatenate([strips, jnp.broadcast_to(notes, (dom, 1, count, width))], axis=1)

    refs = references.reshape(dim_j // 16, 16, pixels)
    share = -(-18 * dim_j // (16 * dom)) * 16
    half = ring // 2
    block = refs.shape
    shifted, part, meta = pl.pallas_call(
        functools.partial(score_kernel, dom, ring),
        out_shape=(
            jax.ShapeDtypeStruct((9 * slots, pixels), jnp.bfloat16),
            jax.ShapeDtypeStruct((dom * share, slots), jnp.float32),
            jax.ShapeDtypeStruct((8, slots), jnp.int32),
        ),
        in_specs=[VMEM] * 2,
        out_specs=(VMEM, VMEM, VMEM),
        scratch_shapes=[
            pltpu.VMEM((ring,) + block, jnp.bfloat16),
            pltpu.VMEM(strips.shape, jnp.bfloat16),
            pltpu.VMEM((pixels, 9 * slots), jnp.bfloat16),
            pltpu.VMEM((2 * dim_j, 9 * slots), jnp.float32),
        ]
        + [sem((half, block[0]))] * 4
        + [sem((dom,)), sem((dom,)), sem((2,))],
        compiler_params=pltpu.CompilerParams(collective_id=0, has_side_effects=True),
    )(refs, strips)

    like, stat = pl.pallas_call(
        functools.partial(evidence_kernel, dom, rotations, 18 * dim_j),
        out_shape=(
            jax.ShapeDtypeStruct((dom, share, slots), jnp.bfloat16),
            jax.ShapeDtypeStruct((dom, 2, slots), jnp.float32),
        ),
        in_specs=[VMEM] * 2,
        out_specs=(VMEM, VMEM),
        scratch_shapes=[pltpu.VMEM((dom // 2, share, slots), jnp.float32)] * 2 + [sem((12, dom // 2))],
        compiler_params=pltpu.CompilerParams(collective_id=1, has_side_effects=True),
    )(part.reshape(dom, share, slots), meta)

    total, evidence = pl.pallas_call(
        functools.partial(sums_kernel, ring),
        out_shape=(
            jax.ShapeDtypeStruct(block, jnp.float32),
            jax.ShapeDtypeStruct((1, count), jnp.float32),
        ),
        in_specs=[VMEM] * 4,
        out_specs=(VMEM, VMEM),
        scratch_shapes=[
            pltpu.VMEM((dom * share, slots), jnp.bfloat16),
            pltpu.VMEM((2 * dim_j, 9 * slots), jnp.bfloat16),
            pltpu.VMEM((ring,) + block, jnp.bfloat16),
        ]
        + [pltpu.VMEM((half,) + block, jnp.bfloat16)] * 2
        + [sem((half, block[0]))] * 4,
        compiler_params=pltpu.CompilerParams(collective_id=2, has_side_effects=True),
    )(like, stat, meta, shifted)
    class_sums = total.reshape(references.shape[0], rotations, pixels).transpose(2, 0, 1)
    return class_sums, evidence.reshape(count)


def solution(mesh):
    placed = (
        P(("dom", "cls"), None, None),
        P(("dom", "cls"), None),
        P(("dom", "cls")),
        P(("dom", "cls"), None),
        P("cls", None, "dom"),
    )
    return jax.shard_map(
        per_device,
        mesh=mesh,
        in_specs=placed,
        out_specs=(P("dom", "cls", None), P(("dom", "cls"))),
        check_vma=False,
    )
```
